32 devices in a mesh: seq: 8 (over z, y), head: 4 (over x, core).
Axes of the slice: x: 2, y: 2, z: 4, core: 2. Of those that a mesh axis runs over, the one named last changes fastest.
Arguments:
- routed_qkv: bfloat16 [3, 2048, 1024], P(None, 'seq', 'head'), may hold values from -64 to 64
- local_qkv: bfloat16 [3, 2048, 3072], P(None, 'seq', 'head'), may hold values from -64 to 64
- cluster_ids: int32 [8, 2048, 1], P('head', 'seq'), may hold values from 0 to 15; in each aligned block of 256 rows (0 to 255, 256 to 511, ..., all dimensions but the last counted through in order) at most 32 rows name the same one
- wo_routed: bfloat16 [1024, 4096], P('head', 'seq'), may hold values from -0.09375 to 0.09375
- wo_local: bfloat16 [3072, 4096], P('head', 'seq'), may hold values from -0.09375 to 0.09375
Outputs:
- layer_out: bfloat16 [2048, 4096], P('seq', 'head')
The draws below stay inside these ranges and needn't reach their ends.
Inputs may be any that keep to these rules, and one draw needn't show every extreme that they name: `cluster_ids`: in each routed head, no cluster holds more than 32 of the 256 tokens of one index of seq (aligned blocks of 256 rows), and some cluster holds exactly 32 of them.
All inputs are finite; a program needn't handle non-finite values.
Results may differ from the reference program's by a relative error of at most 0.0095.
Values may be sent and summed in bfloat16 or wider, within the bound.
No kernel may reach another device: no remote copies, remote signals or barrier semaphores. Data moves between devices by JAX's collectives and lax.ppermute only.
A program may use at most 64 MiB of HBM per device.

```python
import math
import jax
import jax.numpy as jnp
import numpy as np
from jax import lax

D = 4096
HEADS = 32
HD = 128
ROUTED = 8
LOCAL = 24
TOK_DEV = 256
WIN = 256
CLUSTERS = 16
MOST = 32
TOKENS = 2048
N_SEQ = 8
N_HEAD = 4


def make_qkv(key, width):
    base = jax.random.truncated_normal(key, -4.0, 4.0, (3, TOKENS, width), jnp.float32)
    return base.astype(jnp.bfloat16)


def draw_routed_qkv(key, part):
    return make_qkv(jax.random.fold_in(key, 17), ROUTED * HD)


def draw_local_qkv(key, part):
    return make_qkv(jax.random.fold_in(key, 29), LOCAL * HD)


def levels(key, extent, shards, low, high):
    level, own = 1.0, jax.random.fold_in(key, 6)
    for position, parts in shards:
        steps = jnp.exp(jax.random.uniform(jax.random.fold_in(own, position), (parts,), jnp.float32, low / len(shards), high / len(shards)))
        level = level * jnp.repeat(steps, extent[position] // parts).reshape([-1 if axis == position else 1 for axis in range(len(extent))])
    return level


def shared_out(own_key, own, number, rows, count, top, most, skew):
    sequence = jax.random.permutation(own_key, count)
    heavy_load, common = shares(count, rows * top, most, skew, True), shares(count, rows * top, most, skew, False)
    places = jnp.arange(count)

    def named(sizes, offset_by):
        used = int((sizes > 0).sum())
        fixed = max(1, used // 4)
        shifted = fixed + (places - fixed + offset_by * (used - fixed)) % max(1, count - fixed)
        return jnp.zeros((count,), jnp.int32).at[sequence[jnp.where(places < fixed, places, shifted)]].set(jnp.asarray(sizes, jnp.int32))

    sizes = jnp.where(number % 4 == 0, named(heavy_load, number // 4), named(common, number - number // 4 - 1))
    mixed = jax.random.permutation(jax.random.fold_in(own, 3), count)
    donor, sink = mixed[0:count // 2 * 2:2], mixed[1:count // 2 * 2:2]
    margin = jnp.minimum(sizes[donor] - 1, most - sizes[sink]) // 2
    margin = jnp.where((donor == sequence[0]) | (sink == sequence[0]) | (sizes[sink] == 0), 0, jnp.maximum(margin, 0))
    shifted = jax.random.randint(jax.random.fold_in(own, 4), (count // 2,), 0, 1 << 20) % (margin + 1)
    sizes = sizes.at[donor].add(-shifted).at[sink].add(shifted)
    items = jnp.searchsorted(jnp.cumsum(sizes), jnp.arange(rows * top), side="right").astype(jnp.int32)
    grid = items.reshape(top, rows).T
    grid = grid[jax.random.permutation(jax.random.fold_in(own, 1), rows)]
    offset_by = jax.random.randint(jax.random.fold_in(own, 2), (rows, 1), 0, top)
    return jnp.take_along_axis(grid, (jnp.arange(top)[None, :] + offset_by) % top, axis=1)


def shares(amount, total, reach, slope, full):
    weights = [(1 << 20) // math.isqrt(grade ** slope) + 1 for grade in range(1, amount + 1)]
    largest = reach if full else min(reach, max(-(-total // amount), total * weights[0] // sum(weights)))
    least = 1 if total - largest >= amount - 1 else 0
    given, spare = [largest] + [least] * (amount - 1), total - largest - least * (amount - 1)
    while spare > 0:
        movable = [i for i in range(1, amount) if given[i] < largest] or [i for i in range(1, amount) if given[i] < reach]
        whole, left = sum([weights[i] for i in movable]), spare
        for i in movable:
            addition = min(reach - given[i], max(1, left * weights[i] // whole), spare)
            given[i] = given[i] + addition
            spare = spare - addition
    return np.array(given)


def normal_values(own_key, dims, deviation, limit, pieces=(), kind=jnp.bfloat16):
    array = deviation * jax.random.normal(own_key, dims, jnp.float32)
    if pieces:
        array = array * levels(own_key, dims, pieces, -0.22, 0.18)
    return jnp.clip(array, -limit, limit).astype(kind)


def setup_inputs(seed: int = 0) -> dict:
    key_of = jax.random.split(jax.random.key(seed), 6)
    routed_qkv = draw_routed_qkv(jax.random.fold_in(key_of[5], 71), 0)
    local_qkv = draw_local_qkv(jax.random.fold_in(key_of[5], 71), 0)
    cluster_ids_keys = jax.random.split(jax.random.fold_in(key_of[2], 1), ROUTED * TOKENS // TOK_DEV)
    cluster_ids_turns = jax.random.permutation(jax.random.fold_in(key_of[2], 3), ROUTED * TOKENS // TOK_DEV)
    cluster_ids = jax.vmap(lambda own, number: shared_out(jax.random.fold_in(key_of[2], 2), own, number, TOK_DEV, CLUSTERS, 1, MOST, 2))(cluster_ids_keys, cluster_ids_turns).reshape((ROUTED, TOKENS, 1))
    wo_routed = normal_values(key_of[3], (ROUTED * HD, D), (HEADS * HD) ** -0.5, 0.09375, ((0, 4), (1, 8)))
    wo_local = normal_values(key_of[4], (LOCAL * HD, D), (HEADS * HD) ** -0.5, 0.09375, ((0, 4), (1, 8)))
    return dict(routed_qkv=routed_qkv, local_qkv=local_qkv, cluster_ids=cluster_ids, wo_routed=wo_routed, wo_local=wo_local)


def attend(query, keys, values, allowed):
    scores = jnp.einsum('...qd,...kd->...qk', query.astype(jnp.float32), keys.astype(jnp.float32)) * (1.0 / math.sqrt(HD))
    scores = jnp.where(allowed, scores, jnp.float32(-1e+30))
    largest = lax.optimization_barrier(jnp.max(scores, axis=-1, keepdims=True))
    raised = jnp.exp(scores - largest)
    weights = (raised / lax.optimization_barrier(jnp.sum(raised, axis=-1, keepdims=True))).astype(jnp.bfloat16)
    return jnp.einsum('...qk,...kd->...qd', weights.astype(jnp.float32), values.astype(jnp.float32)).astype(jnp.bfloat16)

def routed_head(packed):
    qkv_head, cluster = packed
    blocks = cluster.reshape(N_SEQ, TOK_DEV)
    labels = jnp.arange(CLUSTERS, dtype=jnp.int32)
    onehot = (blocks[:, :, None] == labels[None, None, :]).astype(jnp.int32)
    rank = lax.optimization_barrier(jnp.sum((jnp.cumsum(onehot, axis=1) - 1) * onehot, axis=2))
    source = jnp.arange(N_SEQ, dtype=jnp.int32)[:, None]
    flat = (blocks * (N_SEQ * MOST) + source * MOST + rank).reshape(TOKENS).astype(jnp.int32)
    members = jnp.full((CLUSTERS * N_SEQ * MOST,), -1, jnp.int32).at[flat].set(jnp.arange(TOKENS, dtype=jnp.int32))
    members = members.reshape(CLUSTERS, N_SEQ * MOST)
    safe_ids = jnp.maximum(members, 0)
    query = qkv_head[0][safe_ids]
    keys = qkv_head[1][safe_ids]
    values = qkv_head[2][safe_ids]
    allowed = (members[:, None, :] >= 0) & (members[:, None, :] <= members[:, :, None])
    result = attend(query, keys, values, allowed)
    return result.reshape(CLUSTERS * N_SEQ * MOST, HD)[flat]

def window_stack(values_in, blocks):
    padded = jnp.concatenate([jnp.zeros((WIN, HD), values_in.dtype), values_in], axis=0)
    return jnp.concatenate([padded[:-WIN].reshape(blocks, WIN, HD), values_in.reshape(blocks, WIN, HD)], axis=1)

def local_head(qkv_head):
    blocks = TOKENS // WIN
    query = qkv_head[0].reshape(blocks, WIN, HD)
    keys = window_stack(qkv_head[1], blocks)
    values = window_stack(qkv_head[2], blocks)
    offs_query = jnp.arange(WIN, dtype=jnp.int32)[None, :, None]
    offs_key = jnp.arange(2 * WIN, dtype=jnp.int32)[None, None, :] - WIN
    begins = (jnp.arange(blocks, dtype=jnp.int32) * WIN)[:, None, None]
    allowed = (offs_key <= offs_query) & (offs_key > offs_query - WIN) & (begins + offs_key >= 0)
    return attend(query, keys, values, allowed).reshape(TOKENS, HD)

def reference(routed_qkv, local_qkv, cluster_ids, wo_routed, wo_local):
    routed_heads = routed_qkv.reshape(3, TOKENS, ROUTED, HD).transpose(2, 0, 1, 3)
    routed_attn = lax.map(routed_head, (routed_heads, cluster_ids[:, :, 0]))
    routed_attn = routed_attn.transpose(1, 0, 2).reshape(TOKENS, ROUTED * HD)
    local_heads = local_qkv.reshape(3, TOKENS, LOCAL, HD).transpose(2, 0, 1, 3)
    local_attn = lax.map(local_head, local_heads)
    local_attn = local_attn.transpose(1, 0, 2).reshape(TOKENS, LOCAL * HD)
    routed_cols = ROUTED // N_HEAD * HD
    local_cols = LOCAL // N_HEAD * HD
    total = jnp.zeros((TOKENS, D), jnp.float32)
    for group in range(N_HEAD):
        part_sum = jnp.dot(routed_attn[:, group * routed_cols:(group + 1) * routed_cols], wo_routed[group * routed_cols:(group + 1) * routed_cols], preferred_element_type=jnp.float32)
        part_sum = part_sum + jnp.dot(local_attn[:, group * local_cols:(group + 1) * local_cols], wo_local[group * local_cols:(group + 1) * local_cols], preferred_element_type=jnp.float32)
        total = total + part_sum.astype(jnp.bfloat16).astype(jnp.float32)
    return total.astype(jnp.bfloat16)
```

```python
import math

import jax
import jax.numpy as jnp
from jax import lax
from jax.experimental import pallas as pl
from jax.experimental.pallas import tpu as pltpu
from jax.sharding import PartitionSpec as P

HD = 128
WIN = 256
CL_DEV = 2
LOW = -1e30
SCALE = 1.0 / math.sqrt(HD)


def shifted(block, axis, distance):
    devices = range(lax.axis_size(axis))
    route = [(i - distance, i) for i in devices if i - distance in devices]
    return lax.ppermute(block, axis, route)


def attend(query, keys, values, allowed):
    scores = jnp.einsum("...qd,...kd->...qk", query, keys, preferred_element_type=jnp.float32) * (
        1.0 / math.sqrt(HD)
    )
    scores = jnp.where(allowed, scores, jnp.float32(-1e30))
    largest = jnp.max(scores, axis=-1, keepdims=True)
    raised = jnp.exp(scores - largest)
    weights = (raised / jnp.sum(raised, axis=-1, keepdims=True)).astype(jnp.bfloat16)
    return jnp.einsum(
        "...qk,...kd->...qd", weights, values, preferred_element_type=jnp.float32
    ).astype(jnp.bfloat16)


def general(routed_qkv, local_qkv, cluster_ids, wo_routed, wo_local):
    seq_count = lax.axis_size("seq")
    seq_place = lax.axis_index("seq")
    tok_rows = routed_qkv.shape[1]
    routed_count = cluster_ids.shape[0]
    local_count = local_qkv.shape[2] // HD
    cluster_total = CL_DEV * seq_count
    most_slots = max(2, 2 * tok_rows // cluster_total)
    proj_rows = jnp.concatenate([wo_routed, wo_local], axis=0)
    head_rows = (
        routed_qkv.reshape(3, tok_rows, routed_count, HD)
        .transpose(2, 1, 0, 3)
        .reshape(routed_count, tok_rows, 3 * HD)
    )
    cluster = cluster_ids[:, :, 0]
    labels = jnp.arange(cluster_total, dtype=jnp.int32)
    onehot = (cluster[:, :, None] == labels[None, None, :]).astype(jnp.int32)
    rank = jnp.sum((jnp.cumsum(onehot, axis=1) - 1) * onehot, axis=2)
    slot_index = cluster * most_slots + rank
    own_pos = seq_place * tok_rows + jnp.arange(tok_rows, dtype=jnp.int32)
    slot_total = cluster_total * most_slots

    def place_rows(slot_row, data):
        return jnp.zeros((slot_total, 3 * HD), data.dtype).at[slot_row].set(data)

    def place_pos(slot_row):
        return jnp.full((slot_total,), -1, jnp.int32).at[slot_row].set(own_pos)

    send_rows = jax.vmap(place_rows)(slot_index, head_rows)
    send_pos = jax.vmap(place_pos)(slot_index)
    rows = lax.all_to_all(send_rows, "seq", split_axis=1, concat_axis=1, tiled=True)
    positions = lax.all_to_all(send_pos, "seq", split_axis=1, concat_axis=1, tiled=True)
    count = rows.shape[0]
    slots = rows.shape[1]
    group = seq_count * most_slots
    members = (
        rows.reshape(count, seq_count, CL_DEV, most_slots, 3 * HD)
        .transpose(0, 2, 1, 3, 4)
        .reshape(count, CL_DEV, group, 3 * HD)
    )
    where_at = (
        positions.reshape(count, seq_count, CL_DEV, most_slots)
        .transpose(0, 2, 1, 3)
        .reshape(count, CL_DEV, group)
    )
    allowed = (where_at[..., None, :] >= 0) & (where_at[..., None, :] <= where_at[..., :, None])
    result = attend(members[..., :HD], members[..., HD : 2 * HD], members[..., 2 * HD :], allowed)
    answered = (
        result.reshape(count, CL_DEV, seq_count, most_slots, HD)
        .transpose(0, 2, 1, 3, 4)
        .reshape(count, slots, HD)
    )
    returned = lax.all_to_all(answered, "seq", split_axis=1, concat_axis=1, tiled=True)
    picked = jnp.take_along_axis(returned, slot_index[:, :, None], axis=1)
    routed_attn = picked.transpose(1, 0, 2).reshape(tok_rows, routed_count * HD)
    heads = local_qkv.reshape(3, tok_rows, local_count, HD).transpose(0, 2, 1, 3)
    tail = jnp.stack([heads[1], heads[2]])
    earlier = shifted(tail, "seq", 1)
    keys = jnp.concatenate([earlier[0], heads[1]], axis=1)
    values = jnp.concatenate([earlier[1], heads[2]], axis=1)
    key_pos = seq_place * tok_rows - WIN + jnp.arange(WIN + tok_rows, dtype=jnp.int32)
    query_pos = seq_place * tok_rows + jnp.arange(tok_rows, dtype=jnp.int32)
    allowed = (
        (key_pos[None, :] >= 0)
        & (key_pos[None, :] <= query_pos[:, None])
        & (key_pos[None, :] > query_pos[:, None] - WIN)
    )
    result = attend(heads[0], keys, values, allowed[None])
    local_attn = result.transpose(1, 0, 2).reshape(tok_rows, local_count * HD)
    joined = jnp.concatenate([routed_attn, local_attn], axis=1)
    terms = jnp.dot(
        joined,
        lax.all_gather(proj_rows, "seq", axis=1, tiled=True),
        preferred_element_type=jnp.float32,
    )
    rounded = terms.astype(jnp.bfloat16)
    return (
        lax.psum_scatter(rounded, "head", scatter_dimension=1, tiled=True)
        .astype(jnp.float32)
        .astype(jnp.bfloat16)
    )


AXES = ("seq", "head")


def split_seq(place):
    return place // 4, (place // 2) % 2, place % 2


def moved(block, target):
    route = []
    for place in range(8):
        for head in range(4):
            to = target(place, head)
            if to is not None:
                route.append((place * 4 + head, to[0] * 4 + to[1]))
    return lax.ppermute(block, AXES, route)


def nt(a, b):
    return lax.dot_general(a, b, (((1,), (1,)), ((), ())), preferred_element_type=jnp.float32)


def window_body(first, qkv, tail, out):
    query = qkv[0]
    later = nt(query, qkv[1]) * SCALE
    earlier = nt(query, tail[0]) * SCALE
    row = lax.broadcasted_iota(jnp.int32, later.shape, 0)
    col = lax.broadcasted_iota(jnp.int32, later.shape, 1)
    ahead = col - row
    later = jnp.where(ahead <= 0, later, LOW)
    earlier = jnp.where(ahead > first[0], earlier, LOW)
    top = jnp.maximum(
        jnp.max(later, axis=1, keepdims=True), jnp.max(earlier, axis=1, keepdims=True)
    )
    later = jnp.exp(later - top)
    earlier = jnp.exp(earlier - top)
    total = jnp.sum(later, axis=1, keepdims=True) + jnp.sum(earlier, axis=1, keepdims=True)
    later = (later / total).astype(jnp.bfloat16)
    earlier = (earlier / total).astype(jnp.bfloat16)
    out[...] = (
        jnp.dot(later, qkv[2], preferred_element_type=jnp.float32)
        + jnp.dot(earlier, tail[1], preferred_element_type=jnp.float32)
    ).astype(out.dtype)


def window_heads(local_qkv, tail, is_first):
    rows, width = local_qkv.shape[1:]
    first = jnp.where(is_first, rows, 0).astype(jnp.int32).reshape(1)
    return pl.pallas_call(
        window_body,
        grid_spec=pltpu.PrefetchScalarGridSpec(
            num_scalar_prefetch=1,
            grid=(width // HD,),
            in_specs=[
                pl.BlockSpec((3, rows, HD), lambda i, f: (0, 0, i)),
                pl.BlockSpec((2, rows, HD), lambda i, f: (0, 0, i)),
            ],
            out_specs=pl.BlockSpec((rows, HD), lambda i, f: (0, i)),
        ),
        out_shape=jax.ShapeDtypeStruct((rows, width), jnp.bfloat16),
        name="window_heads",
    )(first, local_qkv, tail)


def routed_body(shift, *refs):
    near, past = refs[:4], refs[4:8]
    out, scores, values = refs[8:]
    rows = out.shape[1]
    row = lax.broadcasted_iota(jnp.int32, (rows, rows), 0)
    col = lax.broadcasted_iota(jnp.int32, (rows, rows), 1)
    gap = row - col

    def names(ref, at):
        two = ref[at : at + 16].astype(jnp.float32)
        turned = jnp.transpose(two)
        along = jnp.concatenate([two[i : i + 1] for i in range(rows // HD)], axis=1)
        down = jnp.concatenate([turned[:, i : i + 1] for i in range(rows // HD)], axis=0)
        return along, down

    near_names = [names(ref, 3 * rows) for ref in near]
    past_names = [names(ref, 2 * rows) for ref in past]
    for j in range(4):
        values[j * rows : (j + 1) * rows] = past[j][rows : 2 * rows]
        values[(4 + j) * rows : (5 + j) * rows] = near[j][2 * rows : 3 * rows]
    for i in range(4):
        query = near[i][0:rows]
        for j in range(8):
            if j < 4:
                keys, along = past[j][0:rows], past_names[j][0]
            else:
                keys, along = near[j - 4][rows : 2 * rows], near_names[j - 4][0]
            allowed = (gap >= shift[i * 8 + j]) & (near_names[i][1] == along)
            scores[:, j * rows : (j + 1) * rows] = jnp.where(allowed, nt(query, keys) * SCALE, LOW)
        raised = scores[...]
        raised = jnp.exp(raised - jnp.max(raised, axis=1, keepdims=True))
        weights = (raised / jnp.sum(raised, axis=1, keepdims=True)).astype(jnp.bfloat16)
        out[i] = jnp.dot(weights, values[...], preferred_element_type=jnp.float32).astype(out.dtype)


def routed_heads(near, past, half, within, rows):
    slots = jnp.array([0, 2, 1, 3], jnp.int32)
    blocks = slots ^ within
    key_at = jnp.concatenate([blocks - 4, blocks])
    shift = (key_at[None, :] - blocks[:, None]) * rows
    never = (jnp.arange(8) < 4)[None, :] & (half == 0)
    shift = jnp.where(never, rows, shift).reshape(32).astype(jnp.int32)
    heads = near[0].shape[1] // HD

    def spec(block):
        return pl.BlockSpec((block.shape[0], HD), lambda i, f: (0, i))

    return pl.pallas_call(
        routed_body,
        grid_spec=pltpu.PrefetchScalarGridSpec(
            num_scalar_prefetch=1,
            grid=(heads,),
            in_specs=[spec(block) for block in (*near, *past)],
            out_specs=pl.BlockSpec((4, rows, HD), lambda i, f: (0, 0, i)),
            scratch_shapes=[
                pltpu.VMEM((rows, 8 * rows), jnp.float32),
                pltpu.VMEM((8 * rows, HD), jnp.bfloat16),
            ],
        ),
        out_shape=jax.ShapeDtypeStruct((4, rows, heads * HD), jnp.bfloat16),
        name="routed_heads",
    )(shift, *near, *past)


def project_body(place, routed, l0, l1, l2, l3, wr0, wl0, wr1, wl1, keep, send):
    width = wr0.shape[1]
    for slot, local in enumerate((l0, l1, l2, l3)):
        halves = []
        for wr, wl in ((wr0, wl0), (wr1, wl1)):
            halves.append(
                (
                    jnp.dot(routed[slot], wr[...], preferred_element_type=jnp.float32)
                    + jnp.dot(local[...], wl[...], preferred_element_type=jnp.float32)
                ).astype(keep.dtype)
            )

        def put(out, at, halves=halves):
            out[at, :, 0:width] = halves[0]
            out[at, :, width:] = halves[1]

        @pl.when(place[slot] == 1)
        def _(put=put, slot=slot):
            put(keep, place[4 + slot])

        @pl.when(place[slot] == 0)
        def _(put=put, slot=slot):
            put(send, place[4 + slot])


def project(place, routed, local, weights):
    rows = routed.shape[1]
    shape = jax.ShapeDtypeStruct((2, rows, 2 * weights[0].shape[1]), jnp.bfloat16)
    whole = pl.BlockSpec(memory_space=pltpu.VMEM)
    return pl.pallas_call(
        project_body,
        in_specs=[pl.BlockSpec(memory_space=pltpu.SMEM)] + [whole] * 9,
        out_specs=(whole, whole),
        out_shape=(shape, shape),
        name="project",
    )(place, routed, *local, *weights)


def block_of_32(routed_qkv, local_qkv, cluster_ids, wo_routed, wo_local):
    place = lax.axis_index("seq")
    head = lax.axis_index("head")
    half, mid, low = split_seq(place)
    far, core = head // 2, head % 2
    rows = routed_qkv.shape[1]
    cols = routed_qkv.shape[2]

    def swap(block, bit):
        return moved(block, lambda s, h: (s ^ bit, h))

    tail = moved(local_qkv[1:], lambda s, h: (s + 1, h) if s < 7 else None)
    names = cluster_ids.reshape(cols // HD, rows // HD, HD).transpose(1, 0, 2).reshape(rows // HD, cols)
    names = jnp.pad(names.astype(jnp.bfloat16), ((0, 16 - rows // HD), (0, 0)))
    own = jnp.concatenate([routed_qkv.reshape(3 * rows, cols), names], axis=0)
    crossed = moved(own[rows:], lambda s, h: (s + 4, h) if s < 4 else None)
    near_mid = swap(own, 2)
    near_low = swap(own, 1)
    near = (own, near_mid, near_low, swap(near_mid, 1))
    past_mid = swap(crossed, 2)
    past_low = swap(crossed, 1)
    past = (crossed, past_mid, past_low, swap(past_mid, 1))
    routed = routed_heads(near, past, half, place % 4, rows)
    other_routed = swap(wo_routed, 4)
    other_local = swap(wo_local, 4)

    result = window_heads(local_qkv, tail, place == 0)
    local_mid = swap(result, 2)
    local = (result, local_mid, swap(result, 1), swap(local_mid, 1))

    slots = jnp.array([0, 2, 1, 3], jnp.int32) ^ (place % 4)
    kept = (slots % 2 == core).astype(jnp.int32)
    order = jnp.concatenate([kept, slots // 2]).astype(jnp.int32)
    keep, send = project(order, routed, local, (wo_routed, wo_local, other_routed, other_local))
    got = moved(send, lambda s, h: (s, h ^ 1))
    both = keep.astype(jnp.float32) + got.astype(jnp.float32)
    width = both.shape[2] // 2
    here = half == far
    mine = jnp.where(here, both[..., :width], both[..., width:])
    theirs = jnp.where(here, both[..., width:], both[..., :width]).astype(jnp.bfloat16)
    total = mine + moved(theirs, lambda s, h: (s, h ^ 2)).astype(jnp.float32)
    total = total.astype(jnp.bfloat16)
    cross = mid == low
    first = jnp.where(cross, total[0], total[1])
    second = jnp.where(cross, total[1], total[0])

    def target(flip):
        def to(s, h):
            r, z, y = split_seq(s)
            return r * 4 + (z ^ y ^ flip) * 2 + h % 2, (h // 2) * 2 + z

        return to

    first = moved(first, target(0))
    second = moved(second, target(1))
    ahead = mid == core
    return jnp.concatenate(
        [jnp.where(ahead, first, second), jnp.where(ahead, second, first)], axis=1
    )


def on_device(*arrays):
    if lax.axis_size("seq") == 8 and lax.axis_size("head") == 4:
        return block_of_32(*arrays)
    return general(*arrays)


def solution(mesh):
    placed = (
        P(None, "seq", "head"),
        P(None, "seq", "head"),
        P("head", "seq", None),
        P("head", "seq"),
        P("head", "seq"),
    )
    return jax.shard_map(
        on_device, mesh=mesh, in_specs=placed, out_specs=P("seq", "head"), check_vma=False
    )
```

```python
import math

import jax
import jax.numpy as jnp
from jax import lax
from jax.experimental import pallas as pl
from jax.experimental.pallas import tpu as pltpu
from jax.sharding import PartitionSpec as P

HD = 128
WIN = 256
CL_DEV = 2
LOW = -1e30
SCALE = 1.0 / math.sqrt(HD)


def shifted(block, axis, distance):
    devices = range(lax.axis_size(axis))
    route = [(i - distance, i) for i in devices if i - distance in devices]
    return lax.ppermute(block, axis, route)


def attend(query, keys, values, allowed):
    scores = jnp.einsum("...qd,...kd->...qk", query, keys, preferred_element_type=jnp.float32) * (
        1.0 / math.sqrt(HD)
    )
    scores = jnp.where(allowed, scores, jnp.float32(-1e30))
    largest = jnp.max(scores, axis=-1, keepdims=True)
    raised = jnp.exp(scores - largest)
    weights = (raised / jnp.sum(raised, axis=-1, keepdims=True)).astype(jnp.bfloat16)
    return jnp.einsum(
        "...qk,...kd->...qd", weights, values, preferred_element_type=jnp.float32
    ).astype(jnp.bfloat16)


def general(routed_qkv, local_qkv, cluster_ids, wo_routed, wo_local):
    seq_count = lax.axis_size("seq")
    seq_place = lax.axis_index("seq")
    tok_rows = routed_qkv.shape[1]
    routed_count = cluster_ids.shape[0]
    local_count = local_qkv.shape[2] // HD
    cluster_total = CL_DEV * seq_count
    most_slots = max(2, 2 * tok_rows // cluster_total)
    proj_rows = jnp.concatenate([wo_routed, wo_local], axis=0)
    head_rows = (
        routed_qkv.reshape(3, tok_rows, routed_count, HD)
        .transpose(2, 1, 0, 3)
        .reshape(routed_count, tok_rows, 3 * HD)
    )
    cluster = cluster_ids[:, :, 0]
    labels = jnp.arange(cluster_total, dtype=jnp.int32)
    onehot = (cluster[:, :, None] == labels[None, None, :]).astype(jnp.int32)
    rank = jnp.sum((jnp.cumsum(onehot, axis=1) - 1) * onehot, axis=2)
    slot_index = cluster * most_slots + rank
    own_pos = seq_place * tok_rows + jnp.arange(tok_rows, dtype=jnp.int32)
    slot_total = cluster_total * most_slots

    def place_rows(slot_row, data):
        return jnp.zeros((slot_total, 3 * HD), data.dtype).at[slot_row].set(data)

    def place_pos(slot_row):
        return jnp.full((slot_total,), -1, jnp.int32).at[slot_row].set(own_pos)

    send_rows = jax.vmap(place_rows)(slot_index, head_rows)
    send_pos = jax.vmap(place_pos)(slot_index)
    rows = lax.all_to_all(send_rows, "seq", split_axis=1, concat_axis=1, tiled=True)
    positions = lax.all_to_all(send_pos, "seq", split_axis=1, concat_axis=1, tiled=True)
    count = rows.shape[0]
    slots = rows.shape[1]
    group = seq_count * most_slots
    members = (
        rows.reshape(count, seq_count, CL_DEV, most_slots, 3 * HD)
        .transpose(0, 2, 1, 3, 4)
        .reshape(count, CL_DEV, group, 3 * HD)
    )
    where_at = (
        positions.reshape(count, seq_count, CL_DEV, most_slots)
        .transpose(0, 2, 1, 3)
        .reshape(count, CL_DEV, group)
    )
    allowed = (where_at[..., None, :] >= 0) & (where_at[..., None, :] <= where_at[..., :, None])
    result = attend(members[..., :HD], members[..., HD : 2 * HD], members[..., 2 * HD :], allowed)
    answered = (
        result.reshape(count, CL_DEV, seq_count, most_slots, HD)
        .transpose(0, 2, 1, 3, 4)
        .reshape(count, slots, HD)
    )
    returned = lax.all_to_all(answered, "seq", split_axis=1, concat_axis=1, tiled=True)
    picked = jnp.take_along_axis(returned, slot_index[:, :, None], axis=1)
    routed_attn = picked.transpose(1, 0, 2).reshape(tok_rows, routed_count * HD)
    heads = local_qkv.reshape(3, tok_rows, local_count, HD).transpose(0, 2, 1, 3)
    tail = jnp.stack([heads[1], heads[2]])
    earlier = shifted(tail, "seq", 1)
    keys = jnp.concatenate([earlier[0], heads[1]], axis=1)
    values = jnp.concatenate([earlier[1], heads[2]], axis=1)
    key_pos = seq_place * tok_rows - WIN + jnp.arange(WIN + tok_rows, dtype=jnp.int32)
    query_pos = seq_place * tok_rows + jnp.arange(tok_rows, dtype=jnp.int32)
    allowed = (
        (key_pos[None, :] >= 0)
        & (key_pos[None, :] <= query_pos[:, None])
        & (key_pos[None, :] > query_pos[:, None] - WIN)
    )
    result = attend(heads[0], keys, values, allowed[None])
    local_attn = result.transpose(1, 0, 2).reshape(tok_rows, local_count * HD)
    joined = jnp.concatenate([routed_attn, local_attn], axis=1)
    terms = jnp.dot(
        joined,
        lax.all_gather(proj_rows, "seq", axis=1, tiled=True),
        preferred_element_type=jnp.float32,
    )
    rounded = terms.astype(jnp.bfloat16)
    return (
        lax.psum_scatter(rounded, "head", scatter_dimension=1, tiled=True)
        .astype(jnp.float32)
        .astype(jnp.bfloat16)
    )


AXES = ("seq", "head")


def split_seq(place):
    return place // 4, (place // 2) % 2, place % 2


def moved(block, target):
    route = []
    for place in range(8):
        for head in range(4):
            to = target(place, head)
            if to is not None:
                route.append((place * 4 + head, to[0] * 4 + to[1]))
    return lax.ppermute(block, AXES, route)


def nt(a, b):
    return lax.dot_general(a, b, (((1,), (1,)), ((), ())), preferred_element_type=jnp.float32)


def after(value, *earlier):
    return lax.optimization_barrier((value, *earlier))[0]


def window_body(first, qkv, tail, out):
    rows = out.shape[0]
    row = lax.broadcasted_iota(jnp.int32, (rows, rows), 0)
    col = lax.broadcasted_iota(jnp.int32, (rows, rows), 1)
    ahead = col - row
    start = first[0]
    for i in range(out.shape[1] // HD):
        at = slice(i * HD, (i + 1) * HD)
        query = qkv[0, :, at]
        later = jnp.where(ahead <= 0, nt(query, qkv[1, :, at]) * SCALE, LOW)
        earlier = jnp.where(ahead > start, nt(query, tail[0, :, at]) * SCALE, LOW)
        top = jnp.max(jnp.maximum(later, earlier), axis=1, keepdims=True)
        later = jnp.exp(later - top)
        earlier = jnp.exp(earlier - top)
        total = jnp.sum(later + earlier, axis=1, keepdims=True)
        mixed = jnp.dot(
            later.astype(jnp.bfloat16), qkv[2, :, at], preferred_element_type=jnp.float32
        ) + jnp.dot(
            earlier.astype(jnp.bfloat16), tail[1, :, at], preferred_element_type=jnp.float32
        )
        out[:, at] = (mixed / total).astype(out.dtype)


WHOLE = pl.BlockSpec(memory_space=pltpu.VMEM)
SCALARS = pl.BlockSpec(memory_space=pltpu.SMEM)


def window_heads(local_qkv, tail, is_first):
    rows, width = local_qkv.shape[1:]
    first = jnp.where(is_first, rows, 0).astype(jnp.int32).reshape(1)
    return pl.pallas_call(
        window_body,
        in_specs=[SCALARS, WHOLE, WHOLE],
        out_specs=WHOLE,
        out_shape=jax.ShapeDtypeStruct((rows, width), jnp.bfloat16),
        name="window_heads",
    )(first, local_qkv, tail)


def names_of(ref, at, e, rows):
    two = ref[at : at + 16, e * HD : (e + 1) * HD].astype(jnp.float32)
    turned = jnp.transpose(two)
    along = jnp.concatenate([two[i : i + 1] for i in range(rows // HD)], axis=1)
    down = jnp.concatenate([turned[:, i : i + 1] for i in range(rows // HD)], axis=0)
    return along, down


def near_body(shift, *refs):
    near, (acc, stat, scores, values) = refs[:4], refs[4:]
    rows = acc.shape[1]
    row = lax.broadcasted_iota(jnp.int32, (rows, rows), 0)
    col = lax.broadcasted_iota(jnp.int32, (rows, rows), 1)
    gap = row - col
    for e in range(acc.shape[2] // HD):
        at = slice(e * HD, (e + 1) * HD)
        names = [names_of(ref, 3 * rows, e, rows) for ref in near]
        for j in range(4):
            values[j * rows : (j + 1) * rows] = near[j][2 * rows : 3 * rows, at]
        for i in range(4):
            query = near[i][0:rows, at]
            for j in range(4):
                allowed = (gap >= shift[i * 4 + j]) & (names[i][1] == names[j][0])
                part = nt(query, near[j][rows : 2 * rows, at]) * SCALE
                scores[:, j * rows : (j + 1) * rows] = jnp.where(allowed, part, LOW)
            raised = scores[...]
            top = jnp.max(raised, axis=1, keepdims=True)
            raised = jnp.exp(raised - top)
            stat[i, :, 2 * e : 2 * e + 1] = top
            stat[i, :, 2 * e + 1 : 2 * e + 2] = jnp.sum(raised, axis=1, keepdims=True)
            acc[i, :, at] = jnp.dot(
                raised.astype(jnp.bfloat16), values[...], preferred_element_type=jnp.float32
            )


def past_body(half, *refs):
    near, past, (acc, stat, out, scores, values) = refs[:4], refs[4:8], refs[8:]
    rows = out.shape[1]

    @pl.when(half[0] == 0)
    def _():
        for e in range(out.shape[2] // HD):
            at = slice(e * HD, (e + 1) * HD)
            for i in range(4):
                total = stat[i, :, 2 * e + 1 : 2 * e + 2]
                out[i, :, at] = (acc[i, :, at] / total).astype(out.dtype)

    @pl.when(half[0] == 1)
    def _():
        for e in range(out.shape[2] // HD):
            at = slice(e * HD, (e + 1) * HD)
            downs = [names_of(ref, 3 * rows, e, rows)[1] for ref in near]
            alongs = [names_of(ref, 2 * rows, e, rows)[0] for ref in past]
            for j in range(4):
                values[j * rows : (j + 1) * rows] = past[j][rows : 2 * rows, at]
            for i in range(4):
                query = near[i][0:rows, at]
                for j in range(4):
                    part = nt(query, past[j][0:rows, at]) * SCALE
                    scores[:, j * rows : (j + 1) * rows] = jnp.where(
                        downs[i] == alongs[j], part, LOW
                    )
                raised = scores[...]
                before = stat[i, :, 2 * e : 2 * e + 1]
                top = jnp.maximum(before, jnp.max(raised, axis=1, keepdims=True))
                raised = jnp.exp(raised - top)
                scaled = jnp.exp(before - top)
                total = scaled * stat[i, :, 2 * e + 1 : 2 * e + 2] + jnp.sum(
                    raised, axis=1, keepdims=True
                )
                mixed = scaled * acc[i, :, at] + jnp.dot(
                    raised.astype(jnp.bfloat16), values[...], preferred_element_type=jnp.float32
                )
                out[i, :, at] = (mixed / total).astype(out.dtype)


def routed_near(near, within, rows):
    blocks = jnp.array([0, 2, 1, 3], jnp.int32) ^ within
    shift = ((blocks[None, :] - blocks[:, None]) * rows).reshape(16).astype(jnp.int32)
    cols = near[0].shape[1]
    return pl.pallas_call(
        near_body,
        in_specs=[SCALARS] + [WHOLE] * 4,
        out_specs=(WHOLE, WHOLE),
        out_shape=(
            jax.ShapeDtypeStruct((4, rows, cols), jnp.float32),
            jax.ShapeDtypeStruct((4, rows, HD), jnp.float32),
        ),
        scratch_shapes=[
            pltpu.VMEM((rows, 4 * rows), jnp.float32),
            pltpu.VMEM((4 * rows, HD), jnp.bfloat16),
        ],
        name="routed_near",
    )(shift, *near)


def routed_past(half, near, past, acc, stat):
    rows, cols = acc.shape[1:]
    return pl.pallas_call(
        past_body,
        in_specs=[SCALARS] + [WHOLE] * 10,
        out_specs=WHOLE,
        out_shape=jax.ShapeDtypeStruct((4, rows, cols), jnp.bfloat16),
        scratch_shapes=[
            pltpu.VMEM((rows, 4 * rows), jnp.float32),
            pltpu.VMEM((4 * rows, HD), jnp.bfloat16),
        ],
        name="routed_past",
    )(half.astype(jnp.int32).reshape(1), *near, *past, acc, stat)


def project_body(use, routed, l0, l1, l2, l3, wr0, wl0, wr1, wl1, keep, send):
    width = wr0.shape[1]

    def part(slot, local, out):
        for i, (wr, wl) in enumerate(((wr0, wl0), (wr1, wl1))):
            out[:, i * width : (i + 1) * width] = (
                jnp.dot(routed[slot], wr[...], preferred_element_type=jnp.float32)
                + jnp.dot(local[...], wl[...], preferred_element_type=jnp.float32)
            ).astype(out.dtype)

    for slot, local in enumerate((l0, l1, l2, l3)):

        @pl.when(use[slot] == 1)
        def _(slot=slot, local=local):
            part(slot, local, keep)

        @pl.when(use[slot] == 2)
        def _(slot=slot, local=local):
            part(slot, local, send)


def project(use, routed, local, weights):
    shape = jax.ShapeDtypeStruct((routed.shape[1], 2 * weights[0].shape[1]), jnp.bfloat16)
    return pl.pallas_call(
        project_body,
        in_specs=[SCALARS] + [WHOLE] * 9,
        out_specs=(WHOLE, WHOLE),
        out_shape=(shape, shape),
        name="project",
    )(use, routed, *local, *weights)


def block_of_32(routed_qkv, local_qkv, cluster_ids, wo_routed, wo_local):
    place = lax.axis_index("seq")
    head = lax.axis_index("head")
    half, mid, low = split_seq(place)
    far, core = head // 2, head % 2
    rows = routed_qkv.shape[1]
    cols = routed_qkv.shape[2]

    def swap(block, bit):
        return moved(block, lambda s, h: (s ^ bit, h))

    def swap_upper(block, bit):
        return moved(block, lambda s, h: (s ^ bit, h) if s >= 4 else None)

    tail = moved(local_qkv[1:], lambda s, h: (s + 1, h) if s < 7 else None)
    names = cluster_ids.reshape(cols // HD, rows // HD, HD).transpose(1, 0, 2).reshape(rows // HD, cols)
    names = jnp.pad(names.astype(jnp.bfloat16), ((0, 16 - rows // HD), (0, 0)))
    own = jnp.concatenate([routed_qkv.reshape(3 * rows, cols), names], axis=0)
    crossed = moved(own[rows:], lambda s, h: (s + 4, h) if s < 4 else None)
    near_mid = swap(own, 2)
    past_mid = swap_upper(crossed, 2)
    other_local = swap(after(wo_local, crossed), 4)
    other_routed = swap(after(wo_routed, crossed), 4)

    result = window_heads(local_qkv, tail, place == 0)
    near_low = swap(after(own, tail), 1)
    near_both = swap(after(near_mid, tail), 1)
    past_low = swap_upper(after(crossed, tail), 1)
    near = (own, near_mid, near_low, near_both)
    local_mid = swap(result, 2)
    past_both = swap_upper(past_mid, 1)
    past = (crossed, past_mid, past_low, past_both)
    local = (result, local_mid, swap(result, 1), swap(local_mid, 1))
    acc, stat = routed_near(near, place % 4, rows)
    routed = routed_past(half, near, past, acc, stat)

    slots = jnp.array([0, 2, 1, 3], jnp.int32)
    kept = jnp.where(slots % 2 == low ^ core, 1, 2)
    weights = (wo_routed, wo_local, other_routed, other_local)
    here = half == far

    def target(flip):
        def to(s, h):
            r, z, y = split_seq(s)
            return r * 4 + (z ^ y ^ flip) * 2 + h % 2, (h // 2) * 2 + z

        return to

    done = []
    for flip in range(2):
        use = jnp.where(slots // 2 == low ^ flip, kept, 0).astype(jnp.int32)
        keep, send = project(use, routed, local, weights)
        got = moved(send, lambda s, h: (s, h ^ 1))
        both = keep.astype(jnp.float32) + got.astype(jnp.float32)
        width = both.shape[1] // 2
        mine = jnp.where(here, both[:, :width], both[:, width:])
        theirs = jnp.where(here, both[:, width:], both[:, :width]).astype(jnp.bfloat16)
        total = mine + moved(theirs, lambda s, h: (s, h ^ 2)).astype(jnp.float32)
        done.append(moved(total.astype(jnp.bfloat16), target(flip)))
    ahead = mid == core
    return jnp.concatenate(
        [jnp.where(ahead, done[0], done[1]), jnp.where(ahead, done[1], done[0])], axis=1
    )


def on_device(*arrays):
    if lax.axis_size("seq") == 8 and lax.axis_size("head") == 4:
        return block_of_32(*arrays)
    return general(*arrays)


def solution(mesh):
    placed = (
        P(None, "seq", "head"),
        P(None, "seq", "head"),
        P("head", "seq", None),
        P("head", "seq"),
        P("head", "seq"),
    )
    return jax.shard_map(
        on_device, mesh=mesh, in_specs=placed, out_specs=P("seq", "head"), check_vma=False
    )
```

```python
import math

import jax
import jax.numpy as jnp
from jax import lax
from jax.experimental import pallas as pl
from jax.experimental.pallas import tpu as pltpu
from jax.sharding import PartitionSpec as P


HD = 128
WIN = 256
CL_DEV = 2
LOW = -1e30
SCALE = 1.0 / math.sqrt(HD)


def shifted(block, axis, distance):
    devices = range(lax.axis_size(axis))
    route = [(i - distance, i) for i in devices if i - distance in devices]
    return lax.ppermute(block, axis, route)


def attend(query, keys, values, allowed):
    scores = jnp.einsum("...qd,...kd->...qk", query, keys, preferred_element_type=jnp.float32) * (
        1.0 / math.sqrt(HD)
    )
    scores = jnp.where(allowed, scores, jnp.float32(-1e30))
    largest = jnp.max(scores, axis=-1, keepdims=True)
    raised = jnp.exp(scores - largest)
    weights = (raised / jnp.sum(raised, axis=-1, keepdims=True)).astype(jnp.bfloat16)
    return jnp.einsum(
        "...qk,...kd->...qd", weights, values, preferred_element_type=jnp.float32
    ).astype(jnp.bfloat16)


def general(routed_qkv, local_qkv, cluster_ids, wo_routed, wo_local):
    seq_count = lax.axis_size("seq")
    seq_place = lax.axis_index("seq")
    tok_rows = routed_qkv.shape[1]
    routed_count = cluster_ids.shape[0]
    local_count = local_qkv.shape[2] // HD
    cluster_total = CL_DEV * seq_count
    most_slots = max(2, 2 * tok_rows // cluster_total)
    proj_rows = jnp.concatenate([wo_routed, wo_local], axis=0)
    head_rows = (
        routed_qkv.reshape(3, tok_rows, routed_count, HD)
        .transpose(2, 1, 0, 3)
        .reshape(routed_count, tok_rows, 3 * HD)
    )
    cluster = cluster_ids[:, :, 0]
    labels = jnp.arange(cluster_total, dtype=jnp.int32)
    onehot = (cluster[:, :, None] == labels[None, None, :]).astype(jnp.int32)
    rank = jnp.sum((jnp.cumsum(onehot, axis=1) - 1) * onehot, axis=2)
    slot_index = cluster * most_slots + rank
    own_pos = seq_place * tok_rows + jnp.arange(tok_rows, dtype=jnp.int32)
    slot_total = cluster_total * most_slots

    def place_rows(slot_row, data):
        return jnp.zeros((slot_total, 3 * HD), data.dtype).at[slot_row].set(data)

    def place_pos(slot_row):
        return jnp.full((slot_total,), -1, jnp.int32).at[slot_row].set(own_pos)

    send_rows = jax.vmap(place_rows)(slot_index, head_rows)
    send_pos = jax.vmap(place_pos)(slot_index)
    rows = lax.all_to_all(send_rows, "seq", split_axis=1, concat_axis=1, tiled=True)
    positions = lax.all_to_all(send_pos, "seq", split_axis=1, concat_axis=1, tiled=True)
    count = rows.shape[0]
    slots = rows.shape[1]
    group = seq_count * most_slots
    members = (
        rows.reshape(count, seq_count, CL_DEV, most_slots, 3 * HD)
        .transpose(0, 2, 1, 3, 4)
        .reshape(count, CL_DEV, group, 3 * HD)
    )
    where_at = (
        positions.reshape(count, seq_count, CL_DEV, most_slots)
        .transpose(0, 2, 1, 3)
        .reshape(count, CL_DEV, group)
    )
    allowed = (where_at[..., None, :] >= 0) & (where_at[..., None, :] <= where_at[..., :, None])
    result = attend(members[..., :HD], members[..., HD : 2 * HD], members[..., 2 * HD :], allowed)
    answered = (
        result.reshape(count, CL_DEV, seq_count, most_slots, HD)
        .transpose(0, 2, 1, 3, 4)
        .reshape(count, slots, HD)
    )
    returned = lax.all_to_all(answered, "seq", split_axis=1, concat_axis=1, tiled=True)
    picked = jnp.take_along_axis(returned, slot_index[:, :, None], axis=1)
    routed_attn = picked.transpose(1, 0, 2).reshape(tok_rows, routed_count * HD)
    heads = local_qkv.reshape(3, tok_rows, local_count, HD).transpose(0, 2, 1, 3)
    tail = jnp.stack([heads[1], heads[2]])
    earlier = shifted(tail, "seq", 1)
    keys = jnp.concatenate([earlier[0], heads[1]], axis=1)
    values = jnp.concatenate([earlier[1], heads[2]], axis=1)
    key_pos = seq_place * tok_rows - WIN + jnp.arange(WIN + tok_rows, dtype=jnp.int32)
    query_pos = seq_place * tok_rows + jnp.arange(tok_rows, dtype=jnp.int32)
    allowed = (
        (key_pos[None, :] >= 0)
        & (key_pos[None, :] <= query_pos[:, None])
        & (key_pos[None, :] > query_pos[:, None] - WIN)
    )
    result = attend(heads[0], keys, values, allowed[None])
    local_attn = result.transpose(1, 0, 2).reshape(tok_rows, local_count * HD)
    joined = jnp.concatenate([routed_attn, local_attn], axis=1)
    terms = jnp.dot(
        joined,
        lax.all_gather(proj_rows, "seq", axis=1, tiled=True),
        preferred_element_type=jnp.float32,
    )
    rounded = terms.astype(jnp.bfloat16)
    return (
        lax.psum_scatter(rounded, "head", scatter_dimension=1, tiled=True)
        .astype(jnp.float32)
        .astype(jnp.bfloat16)
    )


AXES = ("seq", "head")


def split_seq(place):
    return place // 4, (place // 2) % 2, place % 2


def moved(block, target):
    route = []
    for place in range(8):
        for head in range(4):
            to = target(place, head)
            if to is not None:
                route.append((place * 4 + head, to[0] * 4 + to[1]))
    return lax.ppermute(block, AXES, route)


def nt(a, b):
    return lax.dot_general(a, b, (((1,), (1,)), ((), ())), preferred_element_type=jnp.float32)


def window_body(first, qkv, tail, out):
    rows = out.shape[0]
    row = lax.broadcasted_iota(jnp.int32, (rows, rows), 0)
    col = lax.broadcasted_iota(jnp.int32, (rows, rows), 1)
    ahead = col - row
    start = first[0]
    for i in range(out.shape[1] // HD):
        at = slice(i * HD, (i + 1) * HD)
        query = qkv[0, :, at]
        later = jnp.where(ahead <= 0, nt(query, qkv[1, :, at]) * SCALE, LOW)
        earlier = jnp.where(ahead > start, nt(query, tail[0, :, at]) * SCALE, LOW)
        top = jnp.max(jnp.maximum(later, earlier), axis=1, keepdims=True)
        later = jnp.exp(later - top)
        earlier = jnp.exp(earlier - top)
        total = jnp.sum(later + earlier, axis=1, keepdims=True)
        mixed = jnp.dot(
            later.astype(jnp.bfloat16), qkv[2, :, at], preferred_element_type=jnp.float32
        ) + jnp.dot(
            earlier.astype(jnp.bfloat16), tail[1, :, at], preferred_element_type=jnp.float32
        )
        out[:, at] = (mixed / total).astype(out.dtype)


WHOLE = pl.BlockSpec(memory_space=pltpu.VMEM)
SCALARS = pl.BlockSpec(memory_space=pltpu.SMEM)


def window_heads(local_qkv, tail, is_first):
    rows, width = local_qkv.shape[1:]
    first = jnp.where(is_first, rows, 0).astype(jnp.int32).reshape(1)
    return pl.pallas_call(
        window_body,
        in_specs=[SCALARS] + [WHOLE] * 2,
        out_specs=WHOLE,
        out_shape=jax.ShapeDtypeStruct((rows, width), jnp.bfloat16),
        compiler_params=pltpu.CompilerParams(vmem_limit_bytes=12 << 20),
        name="window_heads",
    )(first, local_qkv, tail)


def names_of(ref, at, e, rows):
    two = ref[at : at + 16, e * HD : (e + 1) * HD].astype(jnp.float32)
    turned = jnp.transpose(two)
    along = jnp.concatenate([two[i : i + 1] for i in range(rows // HD)], axis=1)
    down = jnp.concatenate([turned[:, i : i + 1] for i in range(rows // HD)], axis=0)
    return along, down


def near_body(shift, *refs):
    near, (acc, stat, scores, values) = refs[:4], refs[4:]
    rows = acc.shape[1]
    row = lax.broadcasted_iota(jnp.int32, (rows, rows), 0)
    col = lax.broadcasted_iota(jnp.int32, (rows, rows), 1)
    gap = row - col
    for e in range(acc.shape[2] // HD):
        at = slice(e * HD, (e + 1) * HD)
        names = [names_of(ref, 3 * rows, e, rows) for ref in near]
        for j in range(4):
            values[j * rows : (j + 1) * rows] = near[j][2 * rows : 3 * rows, at]
        for i in range(4):
            query = near[i][0:rows, at]
            for j in range(4):
                allowed = (gap >= shift[i * 4 + j]) & (names[i][1] == names[j][0])
                part = nt(query, near[j][rows : 2 * rows, at]) * SCALE
                scores[:, j * rows : (j + 1) * rows] = jnp.where(allowed, part, LOW)
            raised = scores[...]
            top = jnp.max(raised, axis=1, keepdims=True)
            raised = jnp.exp(raised - top)
            stat[i, :, 2 * e : 2 * e + 1] = top
            stat[i, :, 2 * e + 1 : 2 * e + 2] = jnp.sum(raised, axis=1, keepdims=True)
            acc[i, :, at] = jnp.dot(
                raised.astype(jnp.bfloat16), values[...], preferred_element_type=jnp.float32
            )


def past_body(half, *refs):
    near, past, (acc, stat, out, scores, values) = refs[:4], refs[4:8], refs[8:]
    rows = out.shape[1]

    @pl.when(half[0] == 0)
    def _():
        for e in range(out.shape[2] // HD):
            at = slice(e * HD, (e + 1) * HD)
            for i in range(4):
                total = stat[i, :, 2 * e + 1 : 2 * e + 2]
                out[i, :, at] = (acc[i, :, at] / total).astype(out.dtype)

    @pl.when(half[0] == 1)
    def _():
        for e in range(out.shape[2] // HD):
            at = slice(e * HD, (e + 1) * HD)
            downs = [names_of(ref, 3 * rows, e, rows)[1] for ref in near]
            alongs = [names_of(ref, 2 * rows, e, rows)[0] for ref in past]
            for j in range(4):
                values[j * rows : (j + 1) * rows] = past[j][rows : 2 * rows, at]
            for i in range(4):
                query = near[i][0:rows, at]
                for j in range(4):
                    part = nt(query, past[j][0:rows, at]) * SCALE
                    scores[:, j * rows : (j + 1) * rows] = jnp.where(
                        downs[i] == alongs[j], part, LOW
                    )
                raised = scores[...]
                before = stat[i, :, 2 * e : 2 * e + 1]
                top = jnp.maximum(before, jnp.max(raised, axis=1, keepdims=True))
                raised = jnp.exp(raised - top)
                scaled = jnp.exp(before - top)
                total = scaled * stat[i, :, 2 * e + 1 : 2 * e + 2] + jnp.sum(
                    raised, axis=1, keepdims=True
                )
                mixed = scaled * acc[i, :, at] + jnp.dot(
                    raised.astype(jnp.bfloat16), values[...], preferred_element_type=jnp.float32
                )
                out[i, :, at] = (mixed / total).astype(out.dtype)


def routed_near(near, within, rows):
    blocks = jnp.array([0, 2, 1, 3], jnp.int32) ^ within
    shift = ((blocks[None, :] - blocks[:, None]) * rows).reshape(16).astype(jnp.int32)
    cols = near[0].shape[1]
    return pl.pallas_call(
        near_body,
        in_specs=[SCALARS] + [WHOLE] * 4,
        out_specs=(WHOLE, WHOLE),
        out_shape=(
            jax.ShapeDtypeStruct((4, rows, cols), jnp.float32),
            jax.ShapeDtypeStruct((4, rows, HD), jnp.float32),
        ),
        scratch_shapes=[
            pltpu.VMEM((rows, 4 * rows), jnp.float32),
            pltpu.VMEM((4 * rows, HD), jnp.bfloat16),
        ],
        compiler_params=pltpu.CompilerParams(vmem_limit_bytes=20 << 20),
        name="routed_near",
    )(shift, *near)


def routed_past(half, near, past, acc, stat):
    rows, cols = acc.shape[1:]
    return pl.pallas_call(
        past_body,
        in_specs=[SCALARS] + [WHOLE] * 10,
        out_specs=WHOLE,
        out_shape=jax.ShapeDtypeStruct((4, rows, cols), jnp.bfloat16),
        scratch_shapes=[
            pltpu.VMEM((rows, 4 * rows), jnp.float32),
            pltpu.VMEM((4 * rows, HD), jnp.bfloat16),
        ],
        compiler_params=pltpu.CompilerParams(vmem_limit_bytes=20 << 20),
        name="routed_past",
    )(half.astype(jnp.int32).reshape(1), *near, *past, acc, stat)


def project_body(use, routed, l0, l1, l2, l3, wr0, wl0, wr1, *rest):
    *others, keep, send = rest
    width = wr0.shape[1]
    part = others[0].shape[0]

    def product(a, b):
        return jnp.dot(a, b, preferred_element_type=jnp.float32)

    def fill(slot, local, out):
        mine = product(routed[slot], wr0[...]) + product(local[...], wl0[...])
        out[:, 0:width] = mine.astype(out.dtype)
        theirs = product(routed[slot], wr1[...])
        for i, other in enumerate(others):
            theirs = theirs + product(local[:, i * part : (i + 1) * part], other[...])
        out[:, width:] = theirs.astype(out.dtype)

    for slot, local in enumerate((l0, l1, l2, l3)):

        @pl.when(use[slot] == 1)
        def _(slot=slot, local=local):
            fill(slot, local, keep)

        @pl.when(use[slot] == 2)
        def _(slot=slot, local=local):
            fill(slot, local, send)


def project(use, routed, local, weights):
    shape = jax.ShapeDtypeStruct((routed.shape[1], 2 * weights[0].shape[1]), jnp.bfloat16)
    return pl.pallas_call(
        project_body,
        in_specs=[SCALARS] + [WHOLE] * (5 + len(weights)),
        out_specs=(WHOLE, WHOLE),
        out_shape=(shape, shape),
        compiler_params=pltpu.CompilerParams(vmem_limit_bytes=24 << 20),
        name="project",
    )(use, routed, *local, *weights)


def block_of_32(routed_qkv, local_qkv, cluster_ids, wo_routed, wo_local):
    place = lax.axis_index("seq")
    head = lax.axis_index("head")
    half, mid, low = split_seq(place)
    far, core = head // 2, head % 2
    rows = routed_qkv.shape[1]
    cols = routed_qkv.shape[2]

    def swap(block, bit):
        return moved(block, lambda s, h: (s ^ bit, h))

    def swap_upper(block, bit):
        return moved(block, lambda s, h: (s ^ bit, h) if s >= 4 else None)

    tail = moved(local_qkv[1:], lambda s, h: (s + 1, h) if s < 7 else None)
    names = cluster_ids.reshape(cols // HD, rows // HD, HD).transpose(1, 0, 2).reshape(rows // HD, cols)
    names = jnp.pad(names.astype(jnp.bfloat16), ((0, 16 - rows // HD), (0, 0)))
    own = jnp.concatenate([routed_qkv.reshape(3 * rows, cols), names], axis=0)
    crossed = moved(own[rows:], lambda s, h: (s + 4, h) if s < 4 else None)
    near_mid = swap(own, 2)
    past_mid = swap_upper(crossed, 2)
    past_low = swap_upper(crossed, 1)
    part = routed_qkv.shape[2]
    others = [
        swap(wo_local[i * part : (i + 1) * part], 4)
        for i in range(wo_local.shape[0] // part)
    ]
    other_routed = swap(wo_routed, 4)
    near_both = swap(near_mid, 1)
    near_low = swap(own, 1)
    result = window_heads(local_qkv, tail, place == 0)
    local_mid = swap(result, 2)
    local_low = swap(result, 1)
    past_both = swap_upper(past_mid, 1)
    local_both = swap(local_mid, 1)
    near = (own, near_mid, near_low, near_both)
    past = (crossed, past_mid, past_low, past_both)
    local = (result, local_mid, local_low, local_both)
    acc, stat = routed_near(near, place % 4, rows)
    routed = routed_past(half, near, past, acc, stat)

    slots = jnp.array([0, 2, 1, 3], jnp.int32)
    kept = jnp.where(slots % 2 == low ^ core, 1, 2)
    weights = (wo_routed, wo_local, other_routed, *others)
    here = half == far

    def target(flip):
        def to(s, h):
            r, z, y = split_seq(s)
            return r * 4 + (z ^ y ^ flip) * 2 + h % 2, (h // 2) * 2 + z

        return to

    done = []
    for flip in range(2):
        use = jnp.where(slots // 2 == low ^ flip, kept, 0).astype(jnp.int32)
        keep, send = project(use, routed, local, weights)
        got = moved(send, lambda s, h: (s, h ^ 1))
        both = keep.astype(jnp.float32) + got.astype(jnp.float32)
        width = both.shape[1] // 2
        mine = jnp.where(here, both[:, :width], both[:, width:])
        theirs = jnp.where(here, both[:, width:], both[:, :width]).astype(jnp.bfloat16)
        total = mine + moved(theirs, lambda s, h: (s, h ^ 2)).astype(jnp.float32)
        done.append(moved(total.astype(jnp.bfloat16), target(flip)))
    ahead = mid == core
    return jnp.concatenate(
        [jnp.where(ahead, done[0], done[1]), jnp.where(ahead, done[1], done[0])], axis=1
    )


def on_device(*arrays):
    if lax.axis_size("seq") == 8 and lax.axis_size("head") == 4:
        return block_of_32(*arrays)
    return general(*arrays)


def solution(mesh):
    placed = (
        P(None, "seq", "head"),
        P(None, "seq", "head"),
        P("head", "seq", None),
        P("head", "seq"),
        P("head", "seq"),
    )
    return jax.shard_map(
        on_device, mesh=mesh, in_specs=placed, out_specs=P("seq", "head"), check_vma=False
    )
```

```python
import math

import jax
import jax.numpy as jnp
from jax import lax
from jax.experimental import pallas as pl
from jax.experimental.pallas import tpu as pltpu
from jax.sharding import PartitionSpec as P


HD = 128
WIN = 256
CL_DEV = 2
LOW = -1e30
SCALE = 1.0 / math.sqrt(HD)


def shifted(block, axis, distance):
    devices = range(lax.axis_size(axis))
    route = [(i - distance, i) for i in devices if i - distance in devices]
    return lax.ppermute(block, axis, route)


def attend(query, keys, values, allowed):
    scores = jnp.einsum("...qd,...kd->...qk", query, keys, preferred_element_type=jnp.float32) * (
        1.0 / math.sqrt(HD)
    )
    scores = jnp.where(allowed, scores, jnp.float32(-1e30))
    largest = jnp.max(scores, axis=-1, keepdims=True)
    raised = jnp.exp(scores - largest)
    weights = (raised / jnp.sum(raised, axis=-1, keepdims=True)).astype(jnp.bfloat16)
    return jnp.einsum(
        "...qk,...kd->...qd", weights, values, preferred_element_type=jnp.float32
    ).astype(jnp.bfloat16)


def general(routed_qkv, local_qkv, cluster_ids, wo_routed, wo_local):
    seq_count = lax.axis_size("seq")
    seq_place = lax.axis_index("seq")
    tok_rows = routed_qkv.shape[1]
    routed_count = cluster_ids.shape[0]
    local_count = local_qkv.shape[2] // HD
    cluster_total = CL_DEV * seq_count
    most_slots = max(2, 2 * tok_rows // cluster_total)
    proj_rows = jnp.concatenate([wo_routed, wo_local], axis=0)
    head_rows = (
        routed_qkv.reshape(3, tok_rows, routed_count, HD)
        .transpose(2, 1, 0, 3)
        .reshape(routed_count, tok_rows, 3 * HD)
    )
    cluster = cluster_ids[:, :, 0]
    labels = jnp.arange(cluster_total, dtype=jnp.int32)
    onehot = (cluster[:, :, None] == labels[None, None, :]).astype(jnp.int32)
    rank = jnp.sum((jnp.cumsum(onehot, axis=1) - 1) * onehot, axis=2)
    slot_index = cluster * most_slots + rank
    own_pos = seq_place * tok_rows + jnp.arange(tok_rows, dtype=jnp.int32)
    slot_total = cluster_total * most_slots

    def place_rows(slot_row, data):
        return jnp.zeros((slot_total, 3 * HD), data.dtype).at[slot_row].set(data)

    def place_pos(slot_row):
        return jnp.full((slot_total,), -1, jnp.int32).at[slot_row].set(own_pos)

    send_rows = jax.vmap(place_rows)(slot_index, head_rows)
    send_pos = jax.vmap(place_pos)(slot_index)
    rows = lax.all_to_all(send_rows, "seq", split_axis=1, concat_axis=1, tiled=True)
    positions = lax.all_to_all(send_pos, "seq", split_axis=1, concat_axis=1, tiled=True)
    count = rows.shape[0]
    slots = rows.shape[1]
    group = seq_count * most_slots
    members = (
        rows.reshape(count, seq_count, CL_DEV, most_slots, 3 * HD)
        .transpose(0, 2, 1, 3, 4)
        .reshape(count, CL_DEV, group, 3 * HD)
    )
    where_at = (
        positions.reshape(count, seq_count, CL_DEV, most_slots)
        .transpose(0, 2, 1, 3)
        .reshape(count, CL_DEV, group)
    )
    allowed = (where_at[..., None, :] >= 0) & (where_at[..., None, :] <= where_at[..., :, None])
    result = attend(members[..., :HD], members[..., HD : 2 * HD], members[..., 2 * HD :], allowed)
    answered = (
        result.reshape(count, CL_DEV, seq_count, most_slots, HD)
        .transpose(0, 2, 1, 3, 4)
        .reshape(count, slots, HD)
    )
    returned = lax.all_to_all(answered, "seq", split_axis=1, concat_axis=1, tiled=True)
    picked = jnp.take_along_axis(returned, slot_index[:, :, None], axis=1)
    routed_attn = picked.transpose(1, 0, 2).reshape(tok_rows, routed_count * HD)
    heads = local_qkv.reshape(3, tok_rows, local_count, HD).transpose(0, 2, 1, 3)
    tail = jnp.stack([heads[1], heads[2]])
    earlier = shifted(tail, "seq", 1)
    keys = jnp.concatenate([earlier[0], heads[1]], axis=1)
    values = jnp.concatenate([earlier[1], heads[2]], axis=1)
    key_pos = seq_place * tok_rows - WIN + jnp.arange(WIN + tok_rows, dtype=jnp.int32)
    query_pos = seq_place * tok_rows + jnp.arange(tok_rows, dtype=jnp.int32)
    allowed = (
        (key_pos[None, :] >= 0)
        & (key_pos[None, :] <= query_pos[:, None])
        & (key_pos[None, :] > query_pos[:, None] - WIN)
    )
    result = attend(heads[0], keys, values, allowed[None])
    local_attn = result.transpose(1, 0, 2).reshape(tok_rows, local_count * HD)
    joined = jnp.concatenate([routed_attn, local_attn], axis=1)
    terms = jnp.dot(
        joined,
        lax.all_gather(proj_rows, "seq", axis=1, tiled=True),
        preferred_element_type=jnp.float32,
    )
    rounded = terms.astype(jnp.bfloat16)
    return (
        lax.psum_scatter(rounded, "head", scatter_dimension=1, tiled=True)
        .astype(jnp.float32)
        .astype(jnp.bfloat16)
    )


AXES = ("seq", "head")


def split_seq(place):
    return place // 4, (place // 2) % 2, place % 2


def moved(block, target):
    route = []
    for place in range(8):
        for head in range(4):
            to = target(place, head)
            if to is not None:
                route.append((place * 4 + head, to[0] * 4 + to[1]))
    return lax.ppermute(block, AXES, route)


def nt(a, b):
    return lax.dot_general(a, b, (((1,), (1,)), ((), ())), preferred_element_type=jnp.float32)


def window_body(first, qkv, tail, out):
    rows = out.shape[0]
    row = lax.broadcasted_iota(jnp.int32, (rows, rows), 0)
    col = lax.broadcasted_iota(jnp.int32, (rows, rows), 1)
    ahead = col - row
    start = first[0]
    for i in range(out.shape[1] // HD):
        at = slice(i * HD, (i + 1) * HD)
        query = qkv[0, :, at]
        later = jnp.where(ahead <= 0, nt(query, qkv[1, :, at]) * SCALE, LOW)
        earlier = jnp.where(ahead > start, nt(query, tail[0, :, at]) * SCALE, LOW)
        top = jnp.max(jnp.maximum(later, earlier), axis=1, keepdims=True)
        later = jnp.exp(later - top)
        earlier = jnp.exp(earlier - top)
        total = jnp.sum(later + earlier, axis=1, keepdims=True)
        mixed = jnp.dot(
            later.astype(jnp.bfloat16), qkv[2, :, at], preferred_element_type=jnp.float32
        ) + jnp.dot(
            earlier.astype(jnp.bfloat16), tail[1, :, at], preferred_element_type=jnp.float32
        )
        out[:, at] = (mixed / total).astype(out.dtype)


WHOLE = pl.BlockSpec(memory_space=pltpu.VMEM)
SCALARS = pl.BlockSpec(memory_space=pltpu.SMEM)


def window_heads(local_qkv, tail, is_first):
    rows, width = local_qkv.shape[1:]
    first = jnp.where(is_first, rows, 0).astype(jnp.int32).reshape(1)
    return pl.pallas_call(
        window_body,
        in_specs=[SCALARS] + [WHOLE] * 2,
        out_specs=WHOLE,
        out_shape=jax.ShapeDtypeStruct((rows, width), jnp.bfloat16),
        compiler_params=pltpu.CompilerParams(vmem_limit_bytes=12 << 20),
        name="window_heads",
    )(first, local_qkv, tail)


def names_of(ref, at, e, rows):
    two = ref[at : at + 16, e * HD : (e + 1) * HD].astype(jnp.float32)
    turned = jnp.transpose(two)
    along = jnp.concatenate([two[i : i + 1] for i in range(rows // HD)], axis=1)
    down = jnp.concatenate([turned[:, i : i + 1] for i in range(rows // HD)], axis=0)
    return along, down


def near_body(shift, *refs):
    near, (acc, stat, scores, values) = refs[:4], refs[4:]
    rows = acc.shape[1]
    row = lax.broadcasted_iota(jnp.int32, (rows, rows), 0)
    col = lax.broadcasted_iota(jnp.int32, (rows, rows), 1)
    gap = row - col
    for e in range(acc.shape[2] // HD):
        at = slice(e * HD, (e + 1) * HD)
        names = [names_of(ref, 3 * rows, e, rows) for ref in near]
        for j in range(4):
            values[j * rows : (j + 1) * rows] = near[j][2 * rows : 3 * rows, at]
        for i in range(4):
            query = near[i][0:rows, at]
            for j in range(4):
                allowed = (gap >= shift[i * 4 + j]) & (names[i][1] == names[j][0])
                part = nt(query, near[j][rows : 2 * rows, at]) * SCALE
                scores[:, j * rows : (j + 1) * rows] = jnp.where(allowed, part, LOW)
            raised = scores[...]
            top = jnp.max(raised, axis=1, keepdims=True)
            raised = jnp.exp(raised - top)
            stat[i, :, 2 * e : 2 * e + 1] = top
            stat[i, :, 2 * e + 1 : 2 * e + 2] = jnp.sum(raised, axis=1, keepdims=True)
            acc[i, :, at] = jnp.dot(
                raised.astype(jnp.bfloat16), values[...], preferred_element_type=jnp.float32
            )


def past_body(half, *refs):
    near, past, (acc, stat, out, scores, values) = refs[:4], refs[4:8], refs[8:]
    rows = out.shape[1]

    @pl.when(half[0] == 0)
    def _():
        for e in range(out.shape[2] // HD):
            at = slice(e * HD, (e + 1) * HD)
            for i in range(4):
                total = stat[i, :, 2 * e + 1 : 2 * e + 2]
                out[i, :, at] = (acc[i, :, at] / total).astype(out.dtype)

    @pl.when(half[0] == 1)
    def _():
        for e in range(out.shape[2] // HD):
            at = slice(e * HD, (e + 1) * HD)
            downs = [names_of(ref, 3 * rows, e, rows)[1] for ref in near]
            alongs = [names_of(ref, 2 * rows, e, rows)[0] for ref in past]
            for j in range(4):
                values[j * rows : (j + 1) * rows] = past[j][rows : 2 * rows, at]
            for i in range(4):
                query = near[i][0:rows, at]
                for j in range(4):
                    part = nt(query, past[j][0:rows, at]) * SCALE
                    scores[:, j * rows : (j + 1) * rows] = jnp.where(
                        downs[i] == alongs[j], part, LOW
                    )
                raised = scores[...]
                before = stat[i, :, 2 * e : 2 * e + 1]
                top = jnp.maximum(before, jnp.max(raised, axis=1, keepdims=True))
                raised = jnp.exp(raised - top)
                scaled = jnp.exp(before - top)
                total = scaled * stat[i, :, 2 * e + 1 : 2 * e + 2] + jnp.sum(
                    raised, axis=1, keepdims=True
                )
                mixed = scaled * acc[i, :, at] + jnp.dot(
                    raised.astype(jnp.bfloat16), values[...], preferred_element_type=jnp.float32
                )
                out[i, :, at] = (mixed / total).astype(out.dtype)


def routed_near(near, within, rows):
    blocks = jnp.array([0, 2, 1, 3], jnp.int32) ^ within
    shift = ((blocks[None, :] - blocks[:, None]) * rows).reshape(16).astype(jnp.int32)
    cols = near[0].shape[1]
    return pl.pallas_call(
        near_body,
        in_specs=[SCALARS] + [WHOLE] * 4,
        out_specs=(WHOLE, WHOLE),
        out_shape=(
            jax.ShapeDtypeStruct((4, rows, cols), jnp.float32),
            jax.ShapeDtypeStruct((4, rows, HD), jnp.float32),
        ),
        scratch_shapes=[
            pltpu.VMEM((rows, 4 * rows), jnp.float32),
            pltpu.VMEM((4 * rows, HD), jnp.bfloat16),
        ],
        compiler_params=pltpu.CompilerParams(vmem_limit_bytes=20 << 20),
        name="routed_near",
    )(shift, *near)


def routed_past(half, near, past, acc, stat):
    rows, cols = acc.shape[1:]
    return pl.pallas_call(
        past_body,
        in_specs=[SCALARS] + [WHOLE] * 10,
        out_specs=WHOLE,
        out_shape=jax.ShapeDtypeStruct((4, rows, cols), jnp.bfloat16),
        scratch_shapes=[
            pltpu.VMEM((rows, 4 * rows), jnp.float32),
            pltpu.VMEM((4 * rows, HD), jnp.bfloat16),
        ],
        compiler_params=pltpu.CompilerParams(vmem_limit_bytes=20 << 20),
        name="routed_past",
    )(half.astype(jnp.int32).reshape(1), *near, *past, acc, stat)


def combine_body(here, keep, got, stay, cross):
    width = stay.shape[1]
    own, other = slice(0, width), slice(width, 2 * width)

    def add(at, out):
        total = keep[:, at].astype(jnp.float32) + got[:, at].astype(jnp.float32)
        out[...] = total.astype(out.dtype)

    @pl.when(here[0] == 1)
    def _():
        add(own, stay)
        add(other, cross)

    @pl.when(here[0] == 0)
    def _():
        add(other, stay)
        add(own, cross)


def combine(here, keep, got):
    shape = jax.ShapeDtypeStruct((keep.shape[0], keep.shape[1] // 2), keep.dtype)
    return pl.pallas_call(
        combine_body,
        in_specs=[SCALARS, WHOLE, WHOLE],
        out_specs=(WHOLE, WHOLE),
        out_shape=(shape, shape),
        compiler_params=pltpu.CompilerParams(vmem_limit_bytes=6 << 20),
        name="combine",
    )(here, keep, got)


def finish_body(ahead, s0, c0, s1, c1, out):
    width = s0.shape[1]

    def add(stay, cross, at):
        total = stay[...].astype(jnp.float32) + cross[...].astype(jnp.float32)
        out[:, at : at + width] = total.astype(out.dtype)

    @pl.when(ahead[0] == 1)
    def _():
        add(s0, c0, 0)
        add(s1, c1, width)

    @pl.when(ahead[0] == 0)
    def _():
        add(s0, c0, width)
        add(s1, c1, 0)


def finish(ahead, pieces):
    rows, width = pieces[0].shape
    return pl.pallas_call(
        finish_body,
        in_specs=[SCALARS] + [WHOLE] * 4,
        out_specs=WHOLE,
        out_shape=jax.ShapeDtypeStruct((rows, 2 * width), jnp.bfloat16),
        compiler_params=pltpu.CompilerParams(vmem_limit_bytes=6 << 20),
        name="finish",
    )(ahead, *pieces)


def project_body(use, routed, l0, l1, l2, l3, wr0, wl0, wr1, *rest):
    *others, keep, send = rest
    width = wr0.shape[1]
    part = others[0].shape[0]

    def product(a, b):
        return jnp.dot(a, b, preferred_element_type=jnp.float32)

    def fill(slot, local, out):
        mine = product(routed[slot], wr0[...]) + product(local[...], wl0[...])
        out[:, 0:width] = mine.astype(out.dtype)
        theirs = product(routed[slot], wr1[...])
        for i, other in enumerate(others):
            theirs = theirs + product(local[:, i * part : (i + 1) * part], other[...])
        out[:, width:] = theirs.astype(out.dtype)

    for slot, local in enumerate((l0, l1, l2, l3)):

        @pl.when(use[slot] == 1)
        def _(slot=slot, local=local):
            fill(slot, local, keep)

        @pl.when(use[slot] == 2)
        def _(slot=slot, local=local):
            fill(slot, local, send)


def project(use, routed, local, weights):
    shape = jax.ShapeDtypeStruct((routed.shape[1], 2 * weights[0].shape[1]), jnp.bfloat16)
    return pl.pallas_call(
        project_body,
        in_specs=[SCALARS] + [WHOLE] * (5 + len(weights)),
        out_specs=(WHOLE, WHOLE),
        out_shape=(shape, shape),
        compiler_params=pltpu.CompilerParams(vmem_limit_bytes=24 << 20),
        name="project",
    )(use, routed, *local, *weights)


def block_of_32(routed_qkv, local_qkv, cluster_ids, wo_routed, wo_local):
    place = lax.axis_index("seq")
    head = lax.axis_index("head")
    half, mid, low = split_seq(place)
    far, core = head // 2, head % 2
    rows = routed_qkv.shape[1]
    cols = routed_qkv.shape[2]

    def swap(block, bit):
        return moved(block, lambda s, h: (s ^ bit, h))

    def swap_upper(block, bit):
        return moved(block, lambda s, h: (s ^ bit, h) if s >= 4 else None)

    tail = moved(local_qkv[1:], lambda s, h: (s + 1, h) if s < 7 else None)
    names = cluster_ids.reshape(cols // HD, rows // HD, HD).transpose(1, 0, 2).reshape(rows // HD, cols)
    names = jnp.pad(names.astype(jnp.bfloat16), ((0, 16 - rows // HD), (0, 0)))
    own = jnp.concatenate([routed_qkv.reshape(3 * rows, cols), names], axis=0)
    crossed = moved(own[rows:], lambda s, h: (s + 4, h) if s < 4 else None)
    near_mid = swap(own, 2)
    past_mid = swap_upper(crossed, 2)
    past_low = swap_upper(crossed, 1)
    part = routed_qkv.shape[2]
    others = [
        swap(wo_local[i * part : (i + 1) * part], 4)
        for i in range(wo_local.shape[0] // part)
    ]
    other_routed = swap(wo_routed, 4)
    near_both = swap(near_mid, 1)
    near_low = swap(own, 1)
    result = window_heads(local_qkv, tail, place == 0)
    local_mid = swap(result, 2)
    local_low = swap(result, 1)
    past_both = swap_upper(past_mid, 1)
    local_both = swap(local_mid, 1)
    near = (own, near_mid, near_low, near_both)
    past = (crossed, past_mid, past_low, past_both)
    local = (result, local_mid, local_low, local_both)
    acc, stat = routed_near(near, place % 4, rows)
    routed = routed_past(half, near, past, acc, stat)

    slots = jnp.array([0, 2, 1, 3], jnp.int32)
    kept = jnp.where(slots % 2 == low ^ core, 1, 2)
    weights = (wo_routed, wo_local, other_routed, *others)
    here = (half == far).astype(jnp.int32).reshape(1)

    def target(flip, turn):
        def to(s, h):
            r, z, y = split_seq(s)
            return r * 4 + (z ^ y ^ flip) * 2 + h % 2, ((h // 2) ^ turn) * 2 + z

        return to

    pieces = []
    for flip in range(2):
        use = jnp.where(slots // 2 == low ^ flip, kept, 0).astype(jnp.int32)
        keep, send = project(use, routed, local, weights)
        got = moved(send, lambda s, h: (s, h ^ 1))
        stay, cross = combine(here, keep, got)
        cross = moved(cross, target(flip, 1))
        pieces += [moved(stay, target(flip, 0)), cross]
    return finish((mid == core).astype(jnp.int32).reshape(1), pieces)


def on_device(*arrays):
    if lax.axis_size("seq") == 8 and lax.axis_size("head") == 4:
        return block_of_32(*arrays)
    return general(*arrays)


def solution(mesh):
    placed = (
        P(None, "seq", "head"),
        P(None, "seq", "head"),
        P("head", "seq", None),
        P("head", "seq"),
        P("head", "seq"),
    )
    return jax.shard_map(
        on_device, mesh=mesh, in_specs=placed, out_specs=P("seq", "head"), check_vma=False
    )
```

```python
import math

import jax
import jax.numpy as jnp
from jax import lax
from jax.experimental import pallas as pl
from jax.experimental.pallas import tpu as pltpu
from jax.sharding import PartitionSpec as P


HD = 128
WIN = 256
CL_DEV = 2
LOW = -1e30
SCALE = 1.0 / math.sqrt(HD)


def shifted(block, axis, distance):
    devices = range(lax.axis_size(axis))
    route = [(i - distance, i) for i in devices if i - distance in devices]
    return lax.ppermute(block, axis, route)


def attend(query, keys, values, allowed):
    scores = jnp.einsum("...qd,...kd->...qk", query, keys, preferred_element_type=jnp.float32) * (
        1.0 / math.sqrt(HD)
    )
    scores = jnp.where(allowed, scores, jnp.float32(-1e30))
    largest = jnp.max(scores, axis=-1, keepdims=True)
    raised = jnp.exp(scores - largest)
    weights = (raised / jnp.sum(raised, axis=-1, keepdims=True)).astype(jnp.bfloat16)
    return jnp.einsum(
        "...qk,...kd->...qd", weights, values, preferred_element_type=jnp.float32
    ).astype(jnp.bfloat16)


def general(routed_qkv, local_qkv, cluster_ids, wo_routed, wo_local):
    seq_count = lax.axis_size("seq")
    seq_place = lax.axis_index("seq")
    tok_rows = routed_qkv.shape[1]
    routed_count = cluster_ids.shape[0]
    local_count = local_qkv.shape[2] // HD
    cluster_total = CL_DEV * seq_count
    most_slots = max(2, 2 * tok_rows // cluster_total)
    proj_rows = jnp.concatenate([wo_routed, wo_local], axis=0)
    head_rows = (
        routed_qkv.reshape(3, tok_rows, routed_count, HD)
        .transpose(2, 1, 0, 3)
        .reshape(routed_count, tok_rows, 3 * HD)
    )
    cluster = cluster_ids[:, :, 0]
    labels = jnp.arange(cluster_total, dtype=jnp.int32)
    onehot = (cluster[:, :, None] == labels[None, None, :]).astype(jnp.int32)
    rank = jnp.sum((jnp.cumsum(onehot, axis=1) - 1) * onehot, axis=2)
    slot_index = cluster * most_slots + rank
    own_pos = seq_place * tok_rows + jnp.arange(tok_rows, dtype=jnp.int32)
    slot_total = cluster_total * most_slots

    def place_rows(slot_row, data):
        return jnp.zeros((slot_total, 3 * HD), data.dtype).at[slot_row].set(data)

    def place_pos(slot_row):
        return jnp.full((slot_total,), -1, jnp.int32).at[slot_row].set(own_pos)

    send_rows = jax.vmap(place_rows)(slot_index, head_rows)
    send_pos = jax.vmap(place_pos)(slot_index)
    rows = lax.all_to_all(send_rows, "seq", split_axis=1, concat_axis=1, tiled=True)
    positions = lax.all_to_all(send_pos, "seq", split_axis=1, concat_axis=1, tiled=True)
    count = rows.shape[0]
    slots = rows.shape[1]
    group = seq_count * most_slots
    members = (
        rows.reshape(count, seq_count, CL_DEV, most_slots, 3 * HD)
        .transpose(0, 2, 1, 3, 4)
        .reshape(count, CL_DEV, group, 3 * HD)
    )
    where_at = (
        positions.reshape(count, seq_count, CL_DEV, most_slots)
        .transpose(0, 2, 1, 3)
        .reshape(count, CL_DEV, group)
    )
    allowed = (where_at[..., None, :] >= 0) & (where_at[..., None, :] <= where_at[..., :, None])
    result = attend(members[..., :HD], members[..., HD : 2 * HD], members[..., 2 * HD :], allowed)
    answered = (
        result.reshape(count, CL_DEV, seq_count, most_slots, HD)
        .transpose(0, 2, 1, 3, 4)
        .reshape(count, slots, HD)
    )
    returned = lax.all_to_all(answered, "seq", split_axis=1, concat_axis=1, tiled=True)
    picked = jnp.take_along_axis(returned, slot_index[:, :, None], axis=1)
    routed_attn = picked.transpose(1, 0, 2).reshape(tok_rows, routed_count * HD)
    heads = local_qkv.reshape(3, tok_rows, local_count, HD).transpose(0, 2, 1, 3)
    tail = jnp.stack([heads[1], heads[2]])
    earlier = shifted(tail, "seq", 1)
    keys = jnp.concatenate([earlier[0], heads[1]], axis=1)
    values = jnp.concatenate([earlier[1], heads[2]], axis=1)
    key_pos = seq_place * tok_rows - WIN + jnp.arange(WIN + tok_rows, dtype=jnp.int32)
    query_pos = seq_place * tok_rows + jnp.arange(tok_rows, dtype=jnp.int32)
    allowed = (
        (key_pos[None, :] >= 0)
        & (key_pos[None, :] <= query_pos[:, None])
        & (key_pos[None, :] > query_pos[:, None] - WIN)
    )
    result = attend(heads[0], keys, values, allowed[None])
    local_attn = result.transpose(1, 0, 2).reshape(tok_rows, local_count * HD)
    joined = jnp.concatenate([routed_attn, local_attn], axis=1)
    terms = jnp.dot(
        joined,
        lax.all_gather(proj_rows, "seq", axis=1, tiled=True),
        preferred_element_type=jnp.float32,
    )
    rounded = terms.astype(jnp.bfloat16)
    return (
        lax.psum_scatter(rounded, "head", scatter_dimension=1, tiled=True)
        .astype(jnp.float32)
        .astype(jnp.bfloat16)
    )


AXES = ("seq", "head")


def split_seq(place):
    return place // 4, (place // 2) % 2, place % 2


def moved(block, target):
    route = []
    for place in range(8):
        for head in range(4):
            to = target(place, head)
            if to is not None:
                route.append((place * 4 + head, to[0] * 4 + to[1]))
    return lax.ppermute(block, AXES, route)


def nt(a, b):
    return lax.dot_general(a, b, (((1,), (1,)), ((), ())), preferred_element_type=jnp.float32)


def window_body(first, qkv, tail, beside, onward, out, other):
    rows = out.shape[0]
    row = lax.broadcasted_iota(jnp.int32, (rows, rows), 0)
    col = lax.broadcasted_iota(jnp.int32, (rows, rows), 1)
    ahead = col - row
    start = first[0]
    count = out.shape[1] // HD

    @pl.when(first[1] == 1)
    def _():
        other[...] = beside[...]

    @pl.when(first[1] == 0)
    def _():
        other[...] = onward[...]

    for i in range(count):
        at = slice(i * HD, (i + 1) * HD)
        past = tail if i < count // 2 else other
        past_at = slice(i % (count // 2) * HD, (i % (count // 2) + 1) * HD)
        query = qkv[0, :, at]
        later = jnp.where(ahead <= 0, nt(query, qkv[1, :, at]) * SCALE, LOW)
        earlier = jnp.where(ahead > start, nt(query, past[0, :, past_at]) * SCALE, LOW)
        top = jnp.max(jnp.maximum(later, earlier), axis=1, keepdims=True)
        later = jnp.exp(later - top)
        earlier = jnp.exp(earlier - top)
        total = jnp.sum(later + earlier, axis=1, keepdims=True)
        mixed = jnp.dot(
            later.astype(jnp.bfloat16), qkv[2, :, at], preferred_element_type=jnp.float32
        ) + jnp.dot(
            earlier.astype(jnp.bfloat16), past[1, :, past_at], preferred_element_type=jnp.float32
        )
        out[:, at] = (mixed / total).astype(out.dtype)


WHOLE = pl.BlockSpec(memory_space=pltpu.VMEM)
SCALARS = pl.BlockSpec(memory_space=pltpu.SMEM)


def window_heads(local_qkv, tail, beside, onward, low, is_first):
    rows, width = local_qkv.shape[1:]
    first = jnp.stack([jnp.where(is_first, rows, 0), low]).astype(jnp.int32)
    return pl.pallas_call(
        window_body,
        in_specs=[SCALARS] + [WHOLE] * 4,
        out_specs=WHOLE,
        out_shape=jax.ShapeDtypeStruct((rows, width), jnp.bfloat16),
        scratch_shapes=[pltpu.VMEM(tail.shape, tail.dtype)],
        compiler_params=pltpu.CompilerParams(vmem_limit_bytes=8 << 20),
        name="window_heads",
    )(first, local_qkv, tail, beside, onward)


def names_of(ref, at, e, rows):
    two = ref[at : at + 16, e * HD : (e + 1) * HD].astype(jnp.float32)
    turned = jnp.transpose(two)
    along = jnp.concatenate([two[i : i + 1] for i in range(rows // HD)], axis=1)
    down = jnp.concatenate([turned[:, i : i + 1] for i in range(rows // HD)], axis=0)
    return along, down


EARLY = (0, 1, 2)
EARLY_PAST = (0, 2)
LATE_PAST = (1, 3)


def attend_block(query, keys, state, scores, values):
    rows = query.shape[0]
    for j, (key, value, test) in enumerate(keys):
        at = slice(j * rows, (j + 1) * rows)
        values[at] = value
        part = nt(query, key) * SCALE
        scores[:, at] = part if test is None else jnp.where(test(), part, LOW)
    span = len(keys) * rows
    raised = scores[:, 0:span]
    top = jnp.max(raised, axis=1, keepdims=True)
    if state is not None:
        top = jnp.maximum(top, state[0])
    raised = jnp.exp(raised - top)
    total = jnp.sum(raised, axis=1, keepdims=True)
    mixed = jnp.dot(
        raised.astype(jnp.bfloat16), values[0:span], preferred_element_type=jnp.float32
    )
    if state is not None:
        scaled = jnp.exp(state[0] - top)
        total = total + scaled * state[1]
        mixed = mixed + scaled * state[2]
    return top, total, mixed


def key_lists(shift, near, past, e, rows):
    at = slice(e * HD, (e + 1) * HD)
    gap = lax.broadcasted_iota(jnp.int32, (rows, rows), 0) - lax.broadcasted_iota(
        jnp.int32, (rows, rows), 1
    )
    near_names = {j: names_of(ref, 3 * rows, e, rows) for j, ref in near.items()}
    past_names = {j: names_of(ref, 2 * rows, e, rows) for j, ref in past.items()}

    def near_key(i, j):
        test = lambda: (gap >= shift[i * 4 + j]) & (near_names[i][1] == near_names[j][0])
        return near[j][rows : 2 * rows, at], near[j][2 * rows : 3 * rows, at], test

    def past_key(i, j):
        test = lambda: near_names[i][1] == past_names[j][0]
        return past[j][0:rows, at], past[j][rows : 2 * rows, at], test

    return near_key, past_key


def early_body(shift, *refs):
    near = dict(zip(EARLY, refs[:3]))
    past = dict(zip(EARLY_PAST, refs[3:5]))
    acc, stat, scores, values = refs[5:]
    rows = acc.shape[1]

    def run(with_past):
        for e in range(acc.shape[2] // HD):
            at = slice(e * HD, (e + 1) * HD)
            near_key, past_key = key_lists(shift, near, past if with_past else {}, e, rows)
            for i in EARLY:
                keys = [near_key(i, j) for j in EARLY]
                if with_past:
                    keys += [past_key(i, j) for j in EARLY_PAST]
                top, total, mixed = attend_block(near[i][0:rows, at], keys, None, scores, values)
                stat[i, :, 2 * e : 2 * e + 1] = top
                stat[i, :, 2 * e + 1 : 2 * e + 2] = total
                acc[i, :, at] = mixed

    pl.when(shift[16] == 1)(lambda: run(True))
    pl.when(shift[16] == 0)(lambda: run(False))


def late_body(shift, *refs):
    near = dict(enumerate(refs[:4]))
    past = dict(enumerate(refs[4:8]))
    acc, stat, out, scores, values = refs[8:]
    rows = out.shape[1]

    def run(with_past):
        for e in range(out.shape[2] // HD):
            at = slice(e * HD, (e + 1) * HD)
            near_key, past_key = key_lists(shift, near, past if with_past else {}, e, rows)
            for i in range(4):
                early = i in EARLY
                keys = [near_key(i, j) for j in range(4) if not (early and j in EARLY)]
                if with_past:
                    keys += [past_key(i, j) for j in (LATE_PAST if early else range(4))]
                state = None
                if early:
                    state = (
                        stat[i, :, 2 * e : 2 * e + 1],
                        stat[i, :, 2 * e + 1 : 2 * e + 2],
                        acc[i, :, at],
                    )
                _, total, mixed = attend_block(near[i][0:rows, at], keys, state, scores, values)
                out[i, :, at] = (mixed / total).astype(out.dtype)

    pl.when(shift[16] == 1)(lambda: run(True))
    pl.when(shift[16] == 0)(lambda: run(False))


def routed_shift(within, half, rows):
    blocks = jnp.array([0, 2, 1, 3], jnp.int32) ^ within
    shift = ((blocks[None, :] - blocks[:, None]) * rows).reshape(16)
    return jnp.concatenate([shift, half.reshape(1)]).astype(jnp.int32)


def routed_early(shift, near, past, rows):
    cols = near[0].shape[1]
    return pl.pallas_call(
        early_body,
        in_specs=[SCALARS] + [WHOLE] * 5,
        out_specs=(WHOLE, WHOLE),
        out_shape=(
            jax.ShapeDtypeStruct((3, rows, cols), jnp.float32),
            jax.ShapeDtypeStruct((3, rows, HD), jnp.float32),
        ),
        scratch_shapes=[
            pltpu.VMEM((rows, 5 * rows), jnp.float32),
            pltpu.VMEM((5 * rows, HD), jnp.bfloat16),
        ],
        compiler_params=pltpu.CompilerParams(vmem_limit_bytes=12 << 20),
        name="routed_early",
    )(shift, *(near[j] for j in EARLY), *(past[j] for j in EARLY_PAST))


def routed_late(shift, near, past, acc, stat):
    rows, cols = acc.shape[1:]
    return pl.pallas_call(
        late_body,
        in_specs=[SCALARS] + [WHOLE] * 10,
        out_specs=WHOLE,
        out_shape=jax.ShapeDtypeStruct((4, rows, cols), jnp.bfloat16),
        scratch_shapes=[
            pltpu.VMEM((rows, 8 * rows), jnp.float32),
            pltpu.VMEM((8 * rows, HD), jnp.bfloat16),
        ],
        compiler_params=pltpu.CompilerParams(vmem_limit_bytes=16 << 20),
        name="routed_late",
    )(shift, *near, *past, acc, stat)


def combine_body(here, keep, got, stay, cross):
    width = stay.shape[1]
    own, other = slice(0, width), slice(width, 2 * width)

    def add(at, out):
        total = keep[:, at].astype(jnp.float32) + got[:, at].astype(jnp.float32)
        out[...] = total.astype(out.dtype)

    @pl.when(here[0] == 1)
    def _():
        add(own, stay)
        add(other, cross)

    @pl.when(here[0] == 0)
    def _():
        add(other, stay)
        add(own, cross)


def combine(here, keep, got):
    shape = jax.ShapeDtypeStruct((keep.shape[0], keep.shape[1] // 2), keep.dtype)
    return pl.pallas_call(
        combine_body,
        in_specs=[SCALARS, WHOLE, WHOLE],
        out_specs=(WHOLE, WHOLE),
        out_shape=(shape, shape),
        compiler_params=pltpu.CompilerParams(vmem_limit_bytes=4 << 20),
        name="combine",
    )(here, keep, got)


def finish_body(ahead, s0, c0, s1, c1, out):
    width = s0.shape[1]

    def add(stay, cross, at):
        total = stay[...].astype(jnp.float32) + cross[...].astype(jnp.float32)
        out[:, at : at + width] = total.astype(out.dtype)

    @pl.when(ahead[0] == 1)
    def _():
        add(s0, c0, 0)
        add(s1, c1, width)

    @pl.when(ahead[0] == 0)
    def _():
        add(s0, c0, width)
        add(s1, c1, 0)


def finish(ahead, pieces):
    rows, width = pieces[0].shape
    return pl.pallas_call(
        finish_body,
        in_specs=[SCALARS] + [WHOLE] * 4,
        out_specs=WHOLE,
        out_shape=jax.ShapeDtypeStruct((rows, 2 * width), jnp.bfloat16),
        compiler_params=pltpu.CompilerParams(vmem_limit_bytes=4 << 20),
        name="finish",
    )(ahead, *pieces)


def project_body(use, routed, l0, l1, l2, l3, wr0, wl0, wr1, *rest):
    others, outs = rest[:-4], rest[-4:]
    width = wr0.shape[1]
    part = others[0].shape[0]

    def product(a, b):
        return jnp.dot(a, b, preferred_element_type=jnp.float32)

    def fill(slot, local, out):
        mine = product(routed[slot], wr0[...]) + product(local[...], wl0[...])
        out[:, 0:width] = mine.astype(out.dtype)
        theirs = product(routed[slot], wr1[...])
        for i, other in enumerate(others):
            theirs = theirs + product(local[:, i * part : (i + 1) * part], other[...])
        out[:, width:] = theirs.astype(out.dtype)

    for slot, local in enumerate((l0, l1, l2, l3)):
        for k, out in enumerate(outs):

            @pl.when(use[slot] == k)
            def _(slot=slot, local=local, out=out):
                fill(slot, local, out)


def project(use, routed, local, weights):
    shape = jax.ShapeDtypeStruct((routed.shape[1], 2 * weights[0].shape[1]), jnp.bfloat16)
    return pl.pallas_call(
        project_body,
        in_specs=[SCALARS] + [WHOLE] * (5 + len(weights)),
        out_specs=(WHOLE,) * 4,
        out_shape=(shape,) * 4,
        compiler_params=pltpu.CompilerParams(vmem_limit_bytes=16 << 20),
        name="project",
    )(use, routed, *local, *weights)


def block_of_32(routed_qkv, local_qkv, cluster_ids, wo_routed, wo_local):
    place = lax.axis_index("seq")
    head = lax.axis_index("head")
    half, mid, low = split_seq(place)
    far, core = head // 2, head % 2
    rows = routed_qkv.shape[1]
    cols = routed_qkv.shape[2]

    def swap(block, bit):
        return moved(block, lambda s, h: (s ^ bit, h))

    def swap_upper(block, bit):
        return moved(block, lambda s, h: (s ^ bit, h) if s >= 4 else None)

    span = local_qkv.shape[2] // 2
    tail = moved(local_qkv[1:, :, :span], lambda s, h: (s + 1, h) if s < 7 else None)
    others = local_qkv[1:, :, span:]
    tail_b = moved(others, lambda s, h: (s + 1, h) if s % 2 == 0 else None)
    beside = moved(others, lambda s, h: (s - 1, h) if s % 2 == 1 and s < 7 else None)
    onward = moved(beside, lambda s, h: (s + 2, h) if s % 2 == 0 and s < 6 else None)
    names = cluster_ids.reshape(cols // HD, rows // HD, HD).transpose(1, 0, 2).reshape(rows // HD, cols)
    names = jnp.pad(names.astype(jnp.bfloat16), ((0, 16 - rows // HD), (0, 0)))
    own = jnp.concatenate([routed_qkv.reshape(3 * rows, cols), names], axis=0)
    crossed = moved(own[rows:], lambda s, h: (s + 4, h) if s < 4 else None)
    near_mid = swap(own, 2)
    past_mid = swap_upper(crossed, 2)
    past_low = swap_upper(crossed, 1)
    part = routed_qkv.shape[2]
    others = [
        swap(wo_local[i * part : (i + 1) * part], 4)
        for i in range(wo_local.shape[0] // part)
    ]
    other_routed = swap(wo_routed, 4)
    near_both = swap(near_mid, 1)
    near_low = swap(own, 1)
    result = window_heads(local_qkv, tail, tail_b, onward, low, place == 0)
    local_mid = swap(result, 2)
    local_low = swap(result, 1)
    past_both = swap_upper(past_mid, 1)
    local_both = swap(local_mid, 1)
    near = (own, near_mid, near_low, near_both)
    past = (crossed, past_mid, past_low, past_both)
    local = (result, local_mid, local_low, local_both)
    shift = routed_shift(place % 4, half, rows)
    acc, stat = routed_early(shift, near, past, rows)
    routed = routed_late(shift, near, past, acc, stat)

    slots = jnp.array([0, 2, 1, 3], jnp.int32)
    use = 2 * ((slots // 2) ^ low) + ((slots % 2) ^ low ^ core)
    weights = (wo_routed, wo_local, other_routed, *others)
    here = (half == far).astype(jnp.int32).reshape(1)

    def target(flip, turn):
        def to(s, h):
            r, z, y = split_seq(s)
            return r * 4 + (z ^ y ^ flip) * 2 + h % 2, ((h // 2) ^ turn) * 2 + z

        return to

    rows_of = project(use.astype(jnp.int32), routed, local, weights)
    pieces = []
    for flip in range(2):
        keep, send = rows_of[2 * flip : 2 * flip + 2]
        got = moved(send, lambda s, h: (s, h ^ 1))
        stay, cross = combine(here, keep, got)
        cross = moved(cross, target(flip, 1))
        pieces += [moved(stay, target(flip, 0)), cross]
    return finish((mid == core).astype(jnp.int32).reshape(1), pieces)


def on_device(*arrays):
    if lax.axis_size("seq") == 8 and lax.axis_size("head") == 4:
        return block_of_32(*arrays)
    return general(*arrays)


def solution(mesh):
    placed = (
        P(None, "seq", "head"),
        P(None, "seq", "head"),
        P("head", "seq", None),
        P("head", "seq"),
        P("head", "seq"),
    )
    return jax.shard_map(
        on_device, mesh=mesh, in_specs=placed, out_specs=P("seq", "head"), check_vma=False
    )
```
